512 devices in a mesh: row: 16 (over z, core), ma: 32 (over x, y).
Axes of the slice: x: 4, y: 8, z: 8, core: 2. Of those that a mesh axis runs over, the one named last changes fastest.
Arguments:
- toroidal_stream_spectra: float32 [2, 16, 512, 512], P(None, 'row', 'ma'), may hold values from -6 to 6, as said below
- thermal_spectra: float32 [2, 16, 512, 512], P(None, 'row', 'ma'), may hold values from -6 to 6, as said below
- induction_potential: float32 [2, 16, 512, 512], P(None, 'row', 'ma'), may hold values from -6 to 6, as said below
- outward_speed_spectra: float32 [2, 16, 512, 512], P(None, 'row', 'ma'), may hold values from -60 to 60, as said below
- position_azimuth_map: int32 [512], replicated, may hold values from 0 to 511, as said below
- subdiagonal_complement: float32 [2, 16, 512], P(None, 'row'), may hold values from 0.005 to 0.3
- superdiagonal_complement: float32 [2, 16, 512], P(None, 'row'), may hold values from 0.005 to 0.3
- diagonal_entries: float32 [2, 16, 512], P(None, 'row'), may hold values from 2 to 16
Outputs:
- new_temperature: float32 [2, 16, 512, 512], P(None, 'row', 'ma')
- new_magnetic: float32 [2, 16, 512, 512], P(None, 'row', 'ma')
The draws below stay inside these ranges and needn't reach their ends.
Inputs may be any that keep to these rules, and one draw needn't show every extreme that they name: `position_azimuth_map`: slots 2 i and 2 i + 1 hold the orders m and 511 - m; every order stands in exactly one slot. `toroidal_stream_spectra`: an entry whose degree is below the order of its slot in position_azimuth_map is zero. `thermal_spectra`: an entry whose degree is below the order of its slot in position_azimuth_map is zero. `induction_potential`: an entry whose degree is below the order of its slot in position_azimuth_map is zero. `outward_speed_spectra`: an entry whose degree is below the order of its slot in position_azimuth_map is zero.
All inputs are finite; a program needn't handle non-finite values.
Results may differ from the reference program's by a relative error of at most 0.00035.
Values sent between devices are 32-bit elements; how exact they have to be, the bound alone decides.
No kernel may reach another device: no remote copies, remote signals or barrier semaphores. Data moves between devices by JAX's collectives and lax.ppermute only.
A program may use at most 128 MiB of HBM per device.

```python
import math
import jax
import jax.numpy as jnp
from jax import lax

DEGREES = 512
NLAT = 768
NLON = 1536
SHELLS = 16


def slot_orders(key):
    pair_low = jax.random.permutation(jax.random.fold_in(key, 11), DEGREES // 2).astype(jnp.int32)
    partner = DEGREES - 1 - pair_low
    return jnp.stack([pair_low, partner], axis=1).reshape(DEGREES)


def spectrum(key, salt_code, strength):
    orders = slot_orders(key)
    degree_vals = jnp.arange(DEGREES, dtype=jnp.float32)
    live_mask = (degree_vals[None, :] >= orders.astype(jnp.float32)[:, None]).astype(jnp.float32)
    decay_rows = strength / ((1.0 + degree_vals) * jnp.sqrt(1.0 + degree_vals))
    array_shape = (2, SHELLS, DEGREES, DEGREES)
    noise_key = jax.random.fold_in(key, salt_code)
    values = jnp.clip(jax.random.normal(noise_key, array_shape, jnp.float32), -6.0, 6.0)
    return values * decay_rows * live_mask


def draw_position_azimuth_map(key, part):
    return slot_orders(key)


def draw_toroidal_stream_spectra(key, part):
    return spectrum(key, 21, 1.0)


def draw_thermal_spectra(key, part):
    return spectrum(key, 22, 1.0)


def draw_induction_potential(key, part):
    return spectrum(key, 23, 1.0)


def draw_outward_speed_spectra(key, part):
    return spectrum(key, 24, 10.0)


def block_levels(key, extent, shards, low, largest):
    level, own = 1.0, jax.random.fold_in(key, 6)
    for dim, parts in shards:
        heights = jnp.exp(jax.random.uniform(jax.random.fold_in(own, dim), (parts,), jnp.float32, low / len(shards), largest / len(shards)))
        level = level * jnp.repeat(heights, extent[dim] // parts).reshape([-1 if axis == dim else 1 for axis in range(len(extent))])
    return level


def setup_inputs(seed: int = 0) -> dict:
    keys = jax.random.split(jax.random.key(seed), 9)
    toroidal_stream_spectra = draw_toroidal_stream_spectra(jax.random.fold_in(keys[8], 71), 0)
    thermal_spectra = draw_thermal_spectra(jax.random.fold_in(keys[8], 71), 0)
    induction_potential = draw_induction_potential(jax.random.fold_in(keys[8], 71), 0)
    outward_speed_spectra = draw_outward_speed_spectra(jax.random.fold_in(keys[8], 71), 0)
    position_azimuth_map = draw_position_azimuth_map(jax.random.fold_in(keys[8], 71), 0)
    subdiagonal_complement = jnp.clip(jnp.exp(math.log(0.3) - 4.0943446 * jax.random.uniform(keys[5], (2, SHELLS, DEGREES), jnp.float32) ** block_levels(keys[5], (2, SHELLS, DEGREES), ((1, 16),), -0.2, 0.2)), 0.005, 0.3)
    superdiagonal_complement = jnp.clip(jnp.exp(math.log(0.3) - 4.0943446 * jax.random.uniform(keys[6], (2, SHELLS, DEGREES), jnp.float32) ** block_levels(keys[6], (2, SHELLS, DEGREES), ((1, 16),), -0.2, 0.2)), 0.005, 0.3)
    diagonal_entries = jnp.clip(jnp.exp(math.log(16.0) - 2.0794415 * jax.random.uniform(keys[7], (2, SHELLS, DEGREES), jnp.float32) ** block_levels(keys[7], (2, SHELLS, DEGREES), ((1, 16),), -0.2, 0.2)), 2.0, 16.0)
    return dict(toroidal_stream_spectra=toroidal_stream_spectra, thermal_spectra=thermal_spectra, induction_potential=induction_potential, outward_speed_spectra=outward_speed_spectra, position_azimuth_map=position_azimuth_map, subdiagonal_complement=subdiagonal_complement, superdiagonal_complement=superdiagonal_complement, diagonal_entries=diagonal_entries)


inner_radius = 0.35
shell_span = 0.65
time_step = 0.001
highest = lax.Precision.HIGHEST
log_gamma_half = 0.5 * math.log(math.pi) - math.log(2.0)

def legendre_rows(orders, cosine, sine_vals, harmonic_index_array):
    block_len = math.gcd(32, harmonic_index_array)
    dtype_ref = cosine.dtype
    order_col = orders.astype(dtype_ref)[:, None]
    log_start = 0.5 * (lax.lgamma(order_col + 1.5) - lax.lgamma(order_col + 1.0) - log_gamma_half) - 0.5 * math.log(2.0) + order_col * jnp.log(sine_vals)[None, :]
    zero_state = jnp.zeros(log_start.shape, dtype_ref)
    legendre = jnp.zeros((orders.shape[0], harmonic_index_array, cosine.shape[0]), dtype_ref)

    def sweep(position, state_tuple):
        before, current, log_scale, legendre = state_tuple
        new_rows = []
        for offset in range(block_len):
            degree_now = (position * block_len + offset).astype(dtype_ref)
            above_diag = degree_now > order_col
            square = degree_now * degree_now - order_col * order_col
            denominator = jnp.where(above_diag, square, 1.0)
            rise_coef = jnp.where(above_diag, jnp.sqrt(jnp.maximum(4.0 * degree_now * degree_now - 1.0, 1.0) / denominator), 0.0)
            lower_term = (degree_now - 1.0) * (degree_now - 1.0) - order_col * order_col
            fall_coef = jnp.where(above_diag, jnp.sqrt(jnp.maximum((2.0 * degree_now + 1.0) * lower_term, 0.0) / (jnp.maximum(2.0 * degree_now - 3.0, 1.0) * denominator)), 0.0)
            fresh_row = jnp.where(degree_now == order_col, 1.0, rise_coef * cosine[None, :] * current - fall_coef * before)
            before, current = (current, fresh_row)
            new_rows.append(fresh_row * jnp.exp(log_scale))
        magnitude = jnp.maximum(jnp.abs(before), jnp.abs(current))
        magnitude = jnp.where(magnitude > 0.0, magnitude, 1.0)
        before = before / magnitude
        current = current / magnitude
        log_scale = log_scale + jnp.log(magnitude)
        first_row = (position * block_len).astype(jnp.int32)
        legendre = lax.dynamic_update_slice(legendre, jnp.stack(new_rows, axis=1), (jnp.int32(0), first_row, jnp.int32(0)))
        return (before, current, log_scale, legendre)
    state_tuple = lax.fori_loop(0, harmonic_index_array // block_len, sweep, (zero_state, zero_state, log_start, legendre))
    return state_tuple[3]

def wave_table(orders, first_col, column_count, lon_total):
    column_ids = first_col + jnp.arange(column_count, dtype=jnp.int32)
    phase_int = orders[:, None] * column_ids[None, :] % lon_total
    angle_vals = 2.0 * math.pi / lon_total * phase_int.astype(jnp.float32)
    return jnp.stack([jnp.cos(angle_vals), -jnp.sin(angle_vals)], axis=1)

def to_longitudes(spectra, orders, lon_total):
    order_weight = jnp.where(orders == 0, 1.0, 2.0).astype(spectra.dtype)
    weighted = spectra * order_weight[:, None, None, None, None]
    lon_block = math.gcd(512, lon_total)
    output_buf = jnp.zeros((spectra.shape[1], spectra.shape[2], spectra.shape[4], lon_total), spectra.dtype)

    def place(position, output_buf):
        first_col = (position * lon_block).astype(jnp.int32)
        wave_block = wave_table(orders, first_col, lon_block, lon_total).astype(spectra.dtype)
        grid_piece = jnp.einsum('mfscn,mcp->fsnp', weighted, wave_block, precision=highest)
        return lax.dynamic_update_slice(output_buf, grid_piece, (jnp.int32(0), jnp.int32(0), jnp.int32(0), first_col))
    return lax.fori_loop(0, lon_total // lon_block, place, output_buf)

def from_longitudes(grid_sets, orders, lon_total):
    lon_block = math.gcd(512, lon_total)
    running_sum = jnp.zeros((orders.shape[0], grid_sets.shape[0], grid_sets.shape[1], 2, grid_sets.shape[2]), grid_sets.dtype)

    def add_block(position, running_sum):
        first_col = (position * lon_block).astype(jnp.int32)
        wave_block = wave_table(orders, first_col, lon_block, lon_total).astype(grid_sets.dtype)
        grid_piece = lax.dynamic_slice_in_dim(grid_sets, first_col, lon_block, 3)
        return running_sum + jnp.einsum('fsnp,mcp->mfscn', grid_piece, wave_block, precision=highest)
    return lax.fori_loop(0, lon_total // lon_block, add_block, running_sum) / lon_total

def fejer_weights(node_count, lat_total):
    term_count = lat_total // 2
    wave_ints = jnp.arange(1, term_count + 1, dtype=jnp.int32)
    node_ints = 2 * jnp.arange(node_count, dtype=jnp.int32) + 1
    phase_int = wave_ints[:, None] * node_ints[None, :] % (2 * lat_total)
    cosines = jnp.cos(math.pi / lat_total * phase_int.astype(jnp.float32))
    wave_vals = wave_ints.astype(jnp.float32)
    ratio_vals = cosines / (4.0 * wave_vals * wave_vals - 1.0)[:, None]
    return 2.0 / lat_total * (1.0 - 2.0 * lax.optimization_barrier(jnp.sum(ratio_vals, axis=0)))

def nonlinear(grid_sets, factor):
    heat_term = -((grid_sets[3] * grid_sets[1] - grid_sets[0] * grid_sets[4]) * factor + grid_sets[6] * grid_sets[7])
    field_term = -((grid_sets[3] * grid_sets[2] - grid_sets[0] * grid_sets[5]) * factor + grid_sets[6] * grid_sets[8])
    return jnp.stack([heat_term, field_term])

def reference(toroidal_stream_spectra, thermal_spectra, induction_potential, outward_speed_spectra, position_azimuth_map, subdiagonal_complement, superdiagonal_complement, diagonal_entries):
    layer_indices = thermal_spectra.shape[1]
    harmonic_index_array = thermal_spectra.shape[3]
    spacing = shell_span / layer_indices
    order_group = math.gcd(16, harmonic_index_array)
    block_total = harmonic_index_array // order_group
    degree_vals = jnp.arange(harmonic_index_array, dtype=jnp.float32)
    theta_all = math.pi * (jnp.arange(NLAT, dtype=jnp.float32) + 0.5) / NLAT
    cosine_all = jnp.cos(theta_all)
    sine_all = jnp.sin(theta_all)
    order_float = position_azimuth_map.astype(jnp.float32)
    above_diag = degree_vals[None, :] > order_float[:, None]
    link_coef = jnp.where(above_diag, jnp.sqrt(jnp.maximum((2.0 * degree_vals + 1.0) * (degree_vals * degree_vals - order_float[:, None] * order_float[:, None]), 0.0) / jnp.maximum(2.0 * degree_vals - 1.0, 1.0)), 0.0)
    coupled_quantities = jnp.stack([thermal_spectra, induction_potential])
    padded = jnp.pad(coupled_quantities, ((0, 0), (0, 0), (1, 1), (0, 0), (0, 0)))
    depthwise_slope = (padded[:, :, 2:] - padded[:, :, :-2]) / (2.0 * spacing)
    entire_arguments = jnp.stack([toroidal_stream_spectra, thermal_spectra, induction_potential, outward_speed_spectra, depthwise_slope[0], depthwise_slope[1]])

    def synth_block(position):
        first_row = (position * order_group).astype(jnp.int32)
        coef_block = lax.dynamic_slice_in_dim(entire_arguments, first_row, order_group, 3)
        link_block = lax.dynamic_slice_in_dim(link_coef, first_row, order_group, 0)
        orders_block = lax.dynamic_slice_in_dim(order_float, first_row, order_group, 0)
        motion_groupings = coef_block[:3]
        weighted = motion_groupings * degree_vals
        product = motion_groupings * link_block[None, None, None]
        lifted = jnp.concatenate([product[..., 1:], jnp.zeros_like(product[..., :1])], axis=-1)
        coef_sets = jnp.concatenate([motion_groupings, weighted, lifted, coef_block[3:]], axis=0)
        coeffs = jnp.transpose(coef_sets, (3, 0, 2, 1, 4)).reshape(order_group, 12 * layer_indices * 2, harmonic_index_array)
        legendre = legendre_rows(orders_block, cosine_all, sine_all, harmonic_index_array)
        result = jnp.einsum('ocl,oln->ocn', coeffs, legendre, precision=highest).reshape(order_group, 12, layer_indices, 2, NLAT)
        spin_rate = orders_block[:, None, None, None]
        plain_part = result[:, 0:3]
        turned = jnp.stack([-spin_rate * plain_part[:, :, :, 1], spin_rate * plain_part[:, :, :, 0]], axis=3)
        slant_part = cosine_all * result[:, 3:6] - result[:, 6:9]
        return jnp.concatenate([turned, slant_part, result[:, 9:12]], axis=1)
    synth = lax.map(synth_block, jnp.arange(block_total)).reshape(harmonic_index_array, 9, layer_indices, 2, NLAT)

    def shell_step(position):
        shell_now = position.astype(jnp.int32)
        spectra = lax.dynamic_slice_in_dim(synth, shell_now, 1, 2)
        grid_sets = to_longitudes(spectra, position_azimuth_map, NLON)
        radius = inner_radius + spacing * (shell_now.astype(jnp.float32) + 0.5)
        factor = 1.0 / (radius * radius * sine_all * sine_all)
        forcing = nonlinear(grid_sets, factor[None, :, None])
        return from_longitudes(forcing, position_azimuth_map, NLON)
    returned = lax.map(shell_step, jnp.arange(layer_indices))
    returned = jnp.transpose(returned[:, :, :, 0], (1, 2, 0, 3, 4))
    weights = fejer_weights(NLAT, NLAT)
    values = returned.reshape(harmonic_index_array, 4 * layer_indices, NLAT) * weights

    def analysis_block(position):
        first_row = (position * order_group).astype(jnp.int32)
        coef_block = lax.dynamic_slice_in_dim(values, first_row, order_group, 0)
        orders_block = lax.dynamic_slice_in_dim(order_float, first_row, order_group, 0)
        legendre = legendre_rows(orders_block, cosine_all, sine_all, harmonic_index_array)
        return jnp.einsum('ocn,oln->ocl', coef_block, legendre, precision=highest)
    tendency = lax.map(analysis_block, jnp.arange(block_total)).reshape(harmonic_index_array, 2, layer_indices, 2, harmonic_index_array)
    tendency = jnp.transpose(tendency, (1, 3, 2, 0, 4))
    right_side = coupled_quantities + time_step * tendency
    keep_low = 1.0 - subdiagonal_complement
    keep_up = 1.0 - superdiagonal_complement

    def forward(carry_val, shell_data):
        running = shell_data[0] + shell_data[1][:, None, None, :] * carry_val
        return (running, running / shell_data[2][:, None, None, :])
    zero_block = jnp.zeros((2, 2, harmonic_index_array, harmonic_index_array), right_side.dtype)
    last_state, scaled = lax.scan(forward, zero_block, (jnp.moveaxis(right_side, 2, 0), jnp.moveaxis(keep_low, 1, 0), jnp.moveaxis(diagonal_entries, 1, 0)))

    def backward(carry_val, shell_data):
        running = shell_data[0] + shell_data[1][:, None, None, :] * carry_val
        return (running, running)
    last_state, solved = lax.scan(backward, zero_block, (scaled, jnp.moveaxis(keep_up, 1, 0)), reverse=True)
    solved = jnp.moveaxis(solved, 0, 2)
    return (solved[0], solved[1])
```

```python
import math

import jax
import jax.numpy as jnp
import numpy as np
from jax import lax
from jax.experimental import pallas as pl
from jax.experimental.pallas import tpu as pltpu
from jax.sharding import PartitionSpec as P

NLAT = 768
NLON = 1536
NORTH = NLAT // 2
DEG = 512
QUARTER = NLON // 4
GROUP = 16
SHELLS = 16
INNER = 0.35
SPAN = 0.65
STEP = 0.001
RENORM = 32
INTERPRET = False

f32 = jnp.float32
bf16 = jnp.bfloat16
i32 = jnp.int32


def host_tables():
    theta = np.pi * (np.arange(NORTH) + 0.5) / NLAT
    lat = np.zeros((8, NORTH), np.float32)
    lat[0] = np.cos(theta)
    lat[1] = np.log(np.sin(theta))
    orders = np.arange(DEG)
    log_norm = np.array(
        [
            0.5 * (math.lgamma(m + 1.5) - math.lgamma(m + 1.0) - math.lgamma(1.5))
            - 0.5 * math.log(2.0)
            for m in orders
        ]
    )
    norm = np.zeros((8, DEG), np.float32)
    norm[0] = log_norm
    k = np.arange(1, NLAT // 2 + 1)
    weights = (
        2.0
        / NLAT
        * (1.0 - 2.0 * np.sum(np.cos(2.0 * k[:, None] * theta[None]) / (4.0 * k * k - 1.0)[:, None], 0))
    )
    plain = -np.concatenate([weights, weights]) / NLON
    scaled = plain / np.concatenate([np.sin(theta), np.sin(theta)]) ** 2
    per = np.stack([scaled, plain]).reshape(2, 3, 32, 8).transpose(2, 0, 1, 3).reshape(32, 2, 24)
    return lat, norm, per.astype(np.float32)


def split(x):
    high = x.astype(bf16)
    return high, (x - high.astype(f32)).astype(bf16)


def dot_nn(a, b):
    return lax.dot_general(a, b, (((1,), (0,)), ((), ())), preferred_element_type=f32)


def dot_nt(a, b):
    return lax.dot_general(a, b, (((1,), (1,)), ((), ())), preferred_element_type=f32)


def roll_lanes(x, shift):
    return pltpu.roll(x, shift % x.shape[1], 1)


def block_swap(arrays, width):
    arrays = list(arrays)
    count = len(arrays)
    lane = lax.broadcasted_iota(i32, arrays[0].shape, 1) // width
    bit = 1
    while bit < count:
        low = (lane & bit) == 0
        fresh = list(arrays)
        for a in range(count):
            if a & bit == 0:
                b = a | bit
                fresh[a] = jnp.where(low, arrays[a], roll_lanes(arrays[b], bit * width))
                fresh[b] = jnp.where(low, roll_lanes(arrays[a], -bit * width), arrays[b])
        arrays = fresh
        bit *= 2
    return arrays


def pair_slot(map_ref, first, place):
    par = place // 8
    pair = place % 8
    odd = lax.rem(map_ref[first + 2 * pair], 2)
    return 2 * pair + lax.rem(odd + par, 2)


def synthesis_kernel(
    place_ref, map_ref, psi_ref, temp_ref, mag_ref, speed_ref, low_ref, high_ref, lat_ref, norm_ref,
    chunk_ref, high_tab_ref, low_tab_ref, table, coefs, rows,
):
    step = pl.program_id(0)
    first = place_ref[0] * GROUP

    @pl.when(step == 0)
    def _():
        row16 = lax.broadcasted_iota(i32, (GROUP, 128), 0)
        natural = jnp.zeros((GROUP, 128), f32)
        ordered = jnp.zeros((GROUP, 128), f32)
        for s in range(GROUP):
            natural = jnp.where(row16 == s, map_ref[first + s].astype(f32), natural)
            slot = pair_slot(map_ref, first, s)
            ordered = jnp.where(row16 == s, map_ref[first + slot].astype(f32), ordered)
        m = natural[:, :1]
        degree = lax.broadcasted_iota(i32, (GROUP, DEG), 1).astype(f32)
        above = degree > m
        link = jnp.where(
            above,
            jnp.sqrt(
                jnp.maximum((2.0 * degree + 1.0) * (degree * degree - m * m), 0.0)
                / jnp.maximum(2.0 * degree - 1.0, 1.0)
            ),
            0.0,
        )
        weight = jnp.where(m == 0.0, 1.0, 2.0)

        def keep(at, value):
            for t in range(4):
                coefs[t, at * GROUP : (at + 1) * GROUP, :] = value[:, t * 128 : (t + 1) * 128]

        inverse = 1.0 / (2.0 * (SPAN / SHELLS))
        for q, ref in enumerate((psi_ref, temp_ref, mag_ref)):
            for c in range(2):
                value = ref[c * GROUP : (c + 1) * GROUP, :] * weight
                turned = m * value if c == 0 else -m * value
                keep(2 * q + (1 - c), turned)
                keep(6 + 2 * q + c, value * degree)
                keep(12 + 2 * q + c, roll_lanes(value * link, -1))
        for c in range(2):
            part = slice(c * GROUP, (c + 1) * GROUP)
            keep(18 + c, speed_ref[part, :] * weight)
            for q in range(2):
                slope = (high_ref[q, part, :] - low_ref[q, part, :]) * inverse
                keep(20 + 2 * q + c, slope * weight)
        m = ordered[:, :1]
        above = degree > m
        square = degree * degree - m * m
        denominator = jnp.where(above, square, 1.0)
        rise = jnp.where(
            above, jnp.sqrt(jnp.maximum(4.0 * degree * degree - 1.0, 1.0) / denominator), 0.0
        )
        lower = (degree - 1.0) * (degree - 1.0) - m * m
        fall = jnp.where(
            above,
            jnp.sqrt(
                jnp.maximum((2.0 * degree + 1.0) * lower, 0.0)
                / (jnp.maximum(2.0 * degree - 3.0, 1.0) * denominator)
            ),
            0.0,
        )
        log_norm = jnp.sum(jnp.where(degree == m, norm_ref[0:1, :], 0.0), axis=1, keepdims=True)
        x = jnp.broadcast_to(lat_ref[0:1, :], (GROUP, NORTH))
        log_scale = log_norm + m * lat_ref[1:2, :]
        before = jnp.zeros((GROUP, NORTH), f32)
        current = jnp.zeros((GROUP, NORTH), f32)
        order = ordered[:, :1]
        for tile in range(DEG // RENORM):
            scale = jnp.exp(log_scale)
            for l in range(tile * RENORM, (tile + 1) * RENORM):
                fresh = rise[:, l : l + 1] * x * current - fall[:, l : l + 1] * before
                fresh = jnp.where(order == float(l), 1.0, fresh)
                before, current = current, fresh
                value = fresh * scale
                for t in range(3):
                    table[t, l * GROUP : (l + 1) * GROUP, :] = value[:, t * 128 : (t + 1) * 128]
            magnitude = jnp.maximum(jnp.abs(before), jnp.abs(current))
            magnitude = jnp.where(magnitude > 0.0, magnitude, 1.0)
            inverse_magnitude = 1.0 / magnitude
            before = before * inverse_magnitude
            current = current * inverse_magnitude
            log_scale = log_scale + jnp.log(magnitude)

    legendre = jnp.concatenate(
        [table[t, pl.ds(step, DEG, stride=GROUP), :] for t in range(3)], axis=1
    )
    leg_high, leg_low = split(legendre)
    high_tab_ref[0] = leg_high
    low_tab_ref[0] = leg_low

    slot = pair_slot(map_ref, first, step)
    par = step // 8
    north = jnp.concatenate(
        [coefs[t, pl.ds(slot, 24, stride=GROUP), :] for t in range(4)], axis=1
    )
    degree = lax.broadcasted_iota(i32, (24, DEG), 1)
    south = jnp.where(lax.rem(degree + par, 2) == 0, north, -north)
    north_high, north_low = split(north)
    south_high, south_low = split(south)
    high = jnp.concatenate([north_high, south_high], axis=0)
    both = jnp.concatenate([high, north_low, south_low], axis=0)
    first_part = dot_nn(both, leg_high)
    result = first_part[:48] + (first_part[48:] + dot_nn(high, leg_low))
    x = lat_ref[0:1, :]
    base = par * 16 + lax.rem(step, 8)
    for hemi in range(2):
        r = result[24 * hemi : 24 * hemi + 24]
        slant = (x if hemi == 0 else -x) * r[6:12] - r[12:18]
        for q in range(9):
            for c in range(2):
                at = 2 * q + c
                if q < 3:
                    line = r[at : at + 1]
                elif q < 6:
                    line = slant[at - 6 : at - 5]
                else:
                    line = r[at + 6 : at + 7]
                rows[hemi, pl.ds(q * 32 + base + 8 * c, 1), :] = line

    @pl.when(step == GROUP - 1)
    def _():
        for tile in range(2):
            turned = [
                jnp.transpose(rows[h, tile * 128 : (tile + 1) * 128, :]) for h in range(2)
            ]
            turned = jnp.concatenate(turned, axis=0)
            for blk in range(3):
                at = tile * 24 + blk * 8
                chunk_ref[:, at : at + 8, :] = turned[blk * 256 : (blk + 1) * 256].reshape(32, 8, 128)
        rest = jnp.concatenate([rows[0, 256:288, :], rows[1, 256:288, :]], axis=1)
        rest = jnp.concatenate(
            [rest[:, b * 256 : (b + 1) * 256] for b in range(3)] + [jnp.zeros((32, 256), f32)], axis=0
        )
        chunk_ref[:, 48:56, :] = jnp.transpose(rest).reshape(32, 8, 128)


def synthesis(place, orders, psi, temp, mag, speed, low, high, lat, norm):
    whole = lambda *shape: pl.BlockSpec(shape, lambda i: (0,) * len(shape))
    smem = pl.BlockSpec(memory_space=pltpu.SMEM)
    return pl.pallas_call(
        synthesis_kernel,
        grid=(GROUP,),
        in_specs=[smem, smem] + [whole(32, DEG)] * 4 + [whole(2, 32, DEG)] * 2
        + [whole(8, NORTH), whole(8, DEG)],
        out_specs=[
            whole(32, 56, 128),
            pl.BlockSpec((1, DEG, NORTH), lambda i: (i, 0, 0)),
            pl.BlockSpec((1, DEG, NORTH), lambda i: (i, 0, 0)),
        ],
        out_shape=[
            jax.ShapeDtypeStruct((32, 56, 128), f32),
            jax.ShapeDtypeStruct((GROUP, DEG, NORTH), bf16),
            jax.ShapeDtypeStruct((GROUP, DEG, NORTH), bf16),
        ],
        scratch_shapes=[
            pltpu.VMEM((3, DEG * GROUP, 128), f32),
            pltpu.VMEM((4, 24 * GROUP, 128), f32),
            pltpu.VMEM((2, 288, NORTH), f32),
        ],
        interpret=INTERPRET,
        name="synthesis",
    )(place, orders, psi, temp, mag, speed, low, high, lat, norm)


def grid_kernel(x_ref, wave_ref, factor_ref, out_ref, stage):
    for half in range(2):
        lanes = slice(half * 128, (half + 1) * 128)
        for tile in range(2):
            got = block_swap(
                [x_ref[half * 16 + s, tile * 24 : tile * 24 + 24, :] for s in range(16)], 8
            )
            for g in range(16):
                q = tile * 4 + g // 4
                stage[g % 4, q * 24 : (q + 1) * 24, lanes] = got[g]
        got = block_swap([x_ref[half * 16 + s, 48:56, :] for s in range(16)], 8)
        for g in range(12):
            at = 8 * 24 + (g // 4) * 8
            stage[g % 4, at : at + 8, lanes] = got[g]
    tables = [split(wave_ref[pc]) for pc in range(4)]
    waves = []
    for pc in range(4):
        high, low = split(stage[pc])
        wave_high, wave_low = tables[pc]
        waves.append(dot_nn(high, wave_high) + (dot_nn(low, wave_high) + dot_nn(high, wave_low)))
    cos_even, sin_even, cos_odd, sin_odd = waves
    ce, se = cos_even + cos_odd, sin_even + sin_odd
    co, so = cos_even - cos_odd, sin_even - sin_odd
    images = [ce + se, ce - se, co - so, co + so]
    f1 = factor_ref[0:24, :]
    f2 = factor_ref[24:48, :]
    f1 = jnp.concatenate([f1] * 3, axis=1)
    f2 = jnp.concatenate([f2] * 3, axis=1)
    forced = []
    for g in images:
        part = [g[q * 24 : (q + 1) * 24] for q in range(9)]
        heat = (part[3] * part[1] - part[0] * part[4]) * f1 + part[6] * part[7] * f2
        field = (part[3] * part[2] - part[0] * part[5]) * f1 + part[6] * part[8] * f2
        forced.append(jnp.concatenate([heat, field], axis=0))
    a, b = forced[0] + forced[1], forced[2] + forced[3]
    d, e = forced[0] - forced[1], forced[3] - forced[2]
    sides = [a + b, d + e, a - b, d - e]
    for par in range(2):
        parts = []
        for c in range(2):
            pc = par * 2 + c
            high, low = split(sides[pc])
            wave_high, wave_low = tables[pc]
            parts.append(dot_nt(wave_high, high) + (dot_nt(wave_high, low) + dot_nt(wave_low, high)))
        both = jnp.concatenate(parts + [jnp.zeros((256, 32), f32)], axis=1)
        out_ref[:, par * 8 : par * 8 + 8, :] = both.reshape(32, 8, 128)


def grid_stage(x, wave, factor):
    return pl.pallas_call(
        grid_kernel,
        out_shape=jax.ShapeDtypeStruct((32, 16, 128), f32),
        scratch_shapes=[pltpu.VMEM((4, 216, 256), f32)],
        interpret=INTERPRET,
        name="forcing",
    )(x, wave, factor)


def analysis_kernel(
    place_ref, map_ref, v_ref, temp_ref, mag_ref, radial_ref, high_tab_ref, low_tab_ref, out_ref, sums, right
):
    step = pl.program_id(0)
    first = place_ref[0] * GROUP

    @pl.when(step == 0)
    def _():
        for par in range(2):
            halves = [
                block_swap(
                    [v_ref[half * 16 + s, par * 8 : par * 8 + 8, :] for s in range(16)], 8
                )
                for half in range(2)
            ]
            for c in range(2):
                for f in range(2):
                    tiles = []
                    for blk in range(3):
                        g = c * 6 + f * 3 + blk
                        tiles += [halves[0][g], halves[1][g]]
                    for eo in range(2):
                        at = par * 64 + (eo * 4 + f * 2 + c) * 8
                        for t in range(3):
                            mixed = tiles[t] + tiles[t + 3] if eo == 0 else tiles[t] - tiles[t + 3]
                            sums[t, at : at + 8, :] = mixed

    par = step // 8
    slot = pair_slot(map_ref, first, step)
    start = par * 64 + lax.rem(step, 8)
    value = jnp.concatenate(
        [sums[t, pl.ds(start, 8, stride=8), :] for t in range(3)], axis=1
    )
    high, low = split(value)
    leg_high = high_tab_ref[0]
    leg_low = low_tab_ref[0]
    first_part = dot_nt(jnp.concatenate([high, low], axis=0), leg_high)
    result = first_part[:8] + (first_part[8:] + dot_nt(high, leg_low))
    degree = lax.broadcasted_iota(i32, (4, DEG), 1)
    tendency = jnp.where(lax.rem(degree + par, 2) == 0, result[:4], result[4:])
    for fc in range(4):
        right[fc, pl.ds(slot, 1), :] = tendency[fc : fc + 1]

    @pl.when(step == GROUP - 1)
    def _():
        for fc in range(4):
            f, c = fc // 2, fc % 2
            base = temp_ref if f == 0 else mag_ref
            right[fc, 0:GROUP, :] = base[c * GROUP : (c + 1) * GROUP, :] + STEP * right[fc, 0:GROUP, :]
            right[fc, GROUP : GROUP + 8, :] = radial_ref[f]
        for tile in range(4):
            got = block_swap([right[fc, :, tile * 128 : (tile + 1) * 128] for fc in range(4)], 32)
            for r in range(4):
                out_ref[tile * 4 + r] = got[r]


def analysis(place, orders, v, temp, mag, radial, high_tab, low_tab):
    whole = lambda *shape: pl.BlockSpec(shape, lambda i: (0,) * len(shape))
    smem = pl.BlockSpec(memory_space=pltpu.SMEM)
    return pl.pallas_call(
        analysis_kernel,
        grid=(GROUP,),
        in_specs=[smem, smem, whole(32, 16, 128), whole(32, DEG), whole(32, DEG), whole(2, 8, DEG),
                  pl.BlockSpec((1, DEG, NORTH), lambda i: (i, 0, 0)),
                  pl.BlockSpec((1, DEG, NORTH), lambda i: (i, 0, 0))],
        out_specs=whole(16, 24, 128),
        out_shape=jax.ShapeDtypeStruct((16, 24, 128), f32),
        scratch_shapes=[pltpu.VMEM((3, 128, 128), f32), pltpu.VMEM((4, GROUP + 8, DEG), f32)],
        interpret=INTERPRET,
        name="analysis",
    )(place, orders, v, temp, mag, radial, high_tab, low_tab)


def solve_kernel(x_ref, out_ref):
    running = jnp.zeros((GROUP, 128), f32)
    scaled = []
    for k in range(SHELLS):
        running = x_ref[k, 0:GROUP, :] + (1.0 - x_ref[k, GROUP : GROUP + 1, :]) * running
        scaled.append(running / x_ref[k, GROUP + 1 : GROUP + 2, :])
    running = jnp.zeros((GROUP, 128), f32)
    for k in reversed(range(SHELLS)):
        running = scaled[k] + (1.0 - x_ref[k, GROUP + 2 : GROUP + 3, :]) * running
        out_ref[k] = running


def solve(x):
    return pl.pallas_call(
        solve_kernel,
        out_shape=jax.ShapeDtypeStruct((SHELLS, GROUP, 128), f32),
        interpret=INTERPRET,
        name="radial",
    )(x)


def gather_kernel(x_ref, temp_ref, mag_ref):
    for tile in range(4):
        got = block_swap([x_ref[tile * 4 + r] for r in range(4)], 32)
        lanes = slice(tile * 128, (tile + 1) * 128)
        for fc in range(4):
            ref = temp_ref if fc < 2 else mag_ref
            c = fc % 2
            ref[c * GROUP : (c + 1) * GROUP, lanes] = got[fc]


def gather_stage(x):
    return pl.pallas_call(
        gather_kernel,
        out_shape=[jax.ShapeDtypeStruct((32, DEG), f32)] * 2,
        interpret=INTERPRET,
        name="assemble",
    )(x)


def wave_tables(orders):
    pair = orders.reshape(DEG // 2, 2)
    swap = pair[:, :1] % 2 == 1
    pair = jnp.where(swap, pair[:, ::-1], pair)
    node = 2 * jnp.arange(QUARTER, dtype=i32) + 1
    tables = []
    for par in range(2):
        phase = pair[:, par][:, None] * node[None, :] % (2 * NLON)
        angle = math.pi / NLON * phase.astype(f32)
        tables += [jnp.cos(angle), -jnp.sin(angle)]
    return jnp.stack(tables)


def factors(lat_place, shell, per):
    spacing = SPAN / SHELLS
    radius = INNER + spacing * (shell.astype(f32) + 0.5)
    mine = lax.dynamic_index_in_dim(jnp.asarray(per), lat_place, 0, False)
    rows = jnp.concatenate([mine[0] / (radius * radius), mine[1]])
    return jnp.broadcast_to(rows[:, None], (48, 128))


def body(
    toroidal_stream_spectra,
    thermal_spectra,
    induction_potential,
    outward_speed_spectra,
    position_azimuth_map,
    subdiagonal_complement,
    superdiagonal_complement,
    diagonal_entries,
):
    lat, norm, per = host_tables()
    place = lax.axis_index("ma")
    shell = lax.axis_index("row")
    place_array = place.reshape(1).astype(i32)
    flat = lambda a: a.reshape(32, DEG)
    psi, temp, mag, speed = map(
        flat,
        (toroidal_stream_spectra, thermal_spectra, induction_potential, outward_speed_spectra),
    )
    coupled = jnp.stack([temp, mag])
    forward = [(i, i + 1) for i in range(SHELLS - 1)]
    low = lax.ppermute(coupled, "row", forward)
    high = lax.ppermute(coupled, "row", [(b, a) for a, b in forward])
    chunk, high_tab, low_tab = synthesis(
        place_array, position_azimuth_map, psi, temp, mag, speed, low, high, jnp.asarray(lat), jnp.asarray(norm)
    )
    chunk = lax.all_to_all(chunk, "ma", 0, 0, tiled=True)
    spectra = grid_stage(chunk, wave_tables(position_azimuth_map), factors(place, shell, per))
    spectra = lax.all_to_all(spectra, "ma", 0, 0, tiled=True)
    radial = jnp.concatenate(
        [subdiagonal_complement, diagonal_entries, superdiagonal_complement, jnp.zeros((2, 5, DEG), f32)],
        axis=1,
    )
    right = analysis(place_array, position_azimuth_map, spectra, temp, mag, radial, high_tab, low_tab)
    right = lax.all_to_all(right, "row", 0, 0, tiled=True)
    solved = lax.all_to_all(solve(right), "row", 0, 0, tiled=True)
    new_temp, new_mag = gather_stage(solved)
    shape = thermal_spectra.shape
    return new_temp.reshape(shape), new_mag.reshape(shape)


def solution(mesh):
    spectra = P(None, "row", "ma", None)
    radial = P(None, "row", None)
    in_specs = (spectra,) * 4 + (P(),) + (radial,) * 3
    return jax.shard_map(
        body, mesh=mesh, in_specs=in_specs, out_specs=(spectra, spectra), check_vma=False
    )
```

```python
import math

import jax
import jax.numpy as jnp
import numpy as np
from jax import lax
from jax.experimental import pallas as pl
from jax.experimental.pallas import tpu as pltpu
from jax.sharding import PartitionSpec as P

NLAT = 768
NLON = 1536
NORTH = NLAT // 2
DEG = 512
QUARTER = NLON // 4
GROUP = 16
PAIRS = GROUP // 2
UNROLL = 4
SHELLS = 16
INNER = 0.35
SPAN = 0.65
STEP = 0.001
RENORM = 32
INTERPRET = False
ITEMS = [(q, blk) for blk in range(3) for q in (1, 2)] + [
    (q, blk) for q in (0, 3, 4, 5, 6) for blk in range(3)
]

f32 = jnp.float32
bf16 = jnp.bfloat16
i32 = jnp.int32


def host_tables():
    theta = np.pi * (np.arange(NORTH) + 0.5) / NLAT
    lat = np.zeros((8, NORTH), np.float32)
    lat[0] = np.cos(theta)
    lat[1] = np.log(np.sin(theta))
    orders = np.arange(DEG)
    log_norm = np.array(
        [
            0.5 * (math.lgamma(m + 1.5) - math.lgamma(m + 1.0) - math.lgamma(1.5))
            - 0.5 * math.log(2.0)
            for m in orders
        ]
    )
    norm = np.zeros((8, DEG), np.float32)
    norm[0] = log_norm
    k = np.arange(1, NLAT // 2 + 1)
    weights = (
        2.0
        / NLAT
        * (1.0 - 2.0 * np.sum(np.cos(2.0 * k[:, None] * theta[None]) / (4.0 * k * k - 1.0)[:, None], 0))
    )
    plain = -np.concatenate([weights, weights]) / NLON
    scaled = plain / np.concatenate([np.sin(theta), np.sin(theta)]) ** 2
    per = np.zeros((48, 128), np.float32)
    per[:, :32] = np.stack([scaled, plain]).reshape(2, 3, 32, 8).transpose(0, 1, 3, 2).reshape(48, 32)
    return lat, norm, per


def split(x):
    high = x.astype(bf16)
    return high, (x - high.astype(f32)).astype(bf16)


def dot_nn(a, b):
    return lax.dot_general(a, b, (((1,), (0,)), ((), ())), preferred_element_type=f32)


def dot_nt(a, b):
    return lax.dot_general(a, b, (((1,), (1,)), ((), ())), preferred_element_type=f32)


def roll_lanes(x, shift):
    return pltpu.roll(x, shift % x.shape[1], 1)


def block_swap(arrays, width):
    arrays = list(arrays)
    count = len(arrays)
    lane = lax.broadcasted_iota(i32, arrays[0].shape, 1) // width
    bit = 1
    while bit < count:
        low = (lane & bit) == 0
        fresh = list(arrays)
        for a in range(count):
            if a & bit == 0:
                b = a | bit
                fresh[a] = jnp.where(low, arrays[a], roll_lanes(arrays[b], bit * width))
                fresh[b] = jnp.where(low, roll_lanes(arrays[a], -bit * width), arrays[b])
        arrays = fresh
        bit *= 2
    return arrays


def pair_orders(map_ref, first, pair):
    one = map_ref[first + 2 * pair]
    two = map_ref[first + 2 * pair + 1]
    swap = (one > two).astype(i32)
    return 2 * pair + swap, 2 * pair + 1 - swap, jnp.minimum(one, two)


def legendre_table(map_ref, first, lat_ref, norm_ref, table, last):
    row8 = lax.broadcasted_iota(i32, (PAIRS, 128), 0)
    smaller = jnp.zeros((PAIRS, 128), f32)
    for i in range(PAIRS):
        smaller = jnp.where(row8 == i, pair_orders(map_ref, first, i)[2].astype(f32), smaller)
    small = smaller[:, :1]
    place = lax.broadcasted_iota(i32, (PAIRS, DEG + 128), 1).astype(f32)
    front = place <= small
    m = jnp.where(front, DEG - 1.0 - small, small)
    degree = jnp.where(front, DEG - 1.0 - small + place, place - 1.0)
    above = degree > m
    square = degree * degree - m * m
    denominator = jnp.where(above, square, 1.0)
    rise = jnp.where(
        above, jnp.sqrt(jnp.maximum(4.0 * degree * degree - 1.0, 1.0) / denominator), 0.0
    )
    lower = (degree - 1.0) * (degree - 1.0) - m * m
    fall = jnp.where(
        above,
        jnp.sqrt(
            jnp.maximum((2.0 * degree + 1.0) * lower, 0.0)
            / (jnp.maximum(2.0 * degree - 3.0, 1.0) * denominator)
        ),
        0.0,
    )
    wide = lax.broadcasted_iota(i32, (PAIRS, DEG), 1).astype(f32)

    def start(order):
        log_norm = jnp.sum(jnp.where(wide == order, norm_ref[0:1, :], 0.0), axis=1, keepdims=True)
        return log_norm + order * lat_ref[1:2, :]

    x = jnp.broadcast_to(lat_ref[0:1, :], (PAIRS, NORTH))
    log_scale = start(DEG - 1.0 - small)
    log_small = start(small)
    scale_small = jnp.exp(log_small)
    seed = small + 1.0
    before = jnp.zeros((PAIRS, NORTH), f32)
    current = jnp.ones((PAIRS, NORTH), f32)
    for tile in range(DEG // RENORM + 1):
        scale = jnp.exp(log_scale)
        for p in range(tile * RENORM, min((tile + 1) * RENORM, DEG + 1)):
            if p > 0:
                fresh = rise[:, p : p + 1] * x * current - fall[:, p : p + 1] * before
                seeded = seed == float(p)
                fresh = jnp.where(seeded, 1.0, fresh)
                scale = jnp.where(seeded, scale_small, scale)
                before, current = current, fresh
            value = current * scale
            if p < DEG:
                for t in range(3):
                    table[t, p * PAIRS : (p + 1) * PAIRS, :] = value[:, t * 128 : (t + 1) * 128]
            else:
                last[...] = value
        magnitude = jnp.maximum(jnp.abs(before), jnp.abs(current))
        magnitude = jnp.where(magnitude > 0.0, magnitude, 1.0)
        inverse_magnitude = 1.0 / magnitude
        before = before * inverse_magnitude
        current = current * inverse_magnitude
        here = (seed >= float(tile * RENORM)) & (seed < float((tile + 1) * RENORM))
        log_scale = jnp.where(here, log_small, log_scale) + jnp.log(magnitude)


def pair_tile(table, pair, half, t):
    start = half * (DEG // 2) * PAIRS + pair
    high, low = split(table[t, pl.ds(start, DEG // 2, stride=PAIRS), :])
    return jnp.concatenate([high, low], axis=1)


def synthesis_kernel(
    place_ref, map_ref, psi_ref, temp_ref, mag_ref, speed_ref, lat_ref, norm_ref,
    chunk_ref, table, last, coefs, rows,
):
    first = place_ref[0] * GROUP
    legendre_table(map_ref, first, lat_ref, norm_ref, table, last)

    def prepare():
        row16 = lax.broadcasted_iota(i32, (GROUP, 128), 0)
        natural = jnp.zeros((GROUP, 128), f32)
        for s in range(GROUP):
            natural = jnp.where(row16 == s, map_ref[first + s].astype(f32), natural)
        m = natural[:, :1]
        degree = lax.broadcasted_iota(i32, (GROUP, DEG), 1).astype(f32)
        link = jnp.where(
            degree > m,
            jnp.sqrt(
                jnp.maximum((2.0 * degree + 1.0) * (degree * degree - m * m), 0.0)
                / jnp.maximum(2.0 * degree - 1.0, 1.0)
            ),
            0.0,
        )
        weight = jnp.where(m == 0.0, 1.0, 2.0)

        def keep(at, value):
            for t in range(4):
                coefs[t, at * GROUP : (at + 1) * GROUP, :] = value[:, t * 128 : (t + 1) * 128]

        for q, ref in enumerate((psi_ref, temp_ref, mag_ref)):
            for c in range(2):
                value = ref[c * GROUP : (c + 1) * GROUP, :] * weight
                if q == 0:
                    keep(1 - c, m * value if c == 0 else -m * value)
                else:
                    keep(2 * q + c, value)
                keep(6 + 2 * q + c, value * degree)
                keep(12 + 2 * q + c, roll_lanes(value * link, -1))
        for c in range(2):
            keep(18 + c, speed_ref[c * GROUP : (c + 1) * GROUP, :] * weight)
        for at in range(20, 24):
            keep(at, jnp.zeros((GROUP, DEG), f32))

    prepare()

    def one(step):
        final = last[pl.ds(step, 1), :]

        slot_small, slot_large, small = pair_orders(map_ref, first, step)
        par = lax.rem(small, 2)
        wide = lax.broadcasted_iota(i32, (24, DEG), 1)

        def load(slot):
            return jnp.concatenate(
                [coefs[t, pl.ds(slot, 24, stride=GROUP), :] for t in range(4)], axis=1
            )

        plain = load(slot_small)
        edge = plain[:, DEG - 1 :]
        north = jnp.where(wide == 0, 0.0, roll_lanes(plain, 1))
        flip = lax.rem(wide + 1 + par, 2) == 0
        south = jnp.where(flip, north, -north)
        north_large = pltpu.roll(load(slot_large), small + 1, 1)
        south_large = jnp.where(lax.rem(wide, 2) == 0, north_large, -north_large)
        high, low = split(jnp.concatenate([north, south, north_large, south_large], axis=0))
        both = jnp.concatenate([high, low], axis=0)
        thirds = []
        for t in range(3):
            product = dot_nn(both[:, : DEG // 2], pair_tile(table, step, 0, t)) + dot_nn(
                both[:, DEG // 2 :], pair_tile(table, step, 1, t)
            )
            thirds.append(product[:96, :128] + (product[96:, :128] + product[:96, 128:]))
        result = jnp.concatenate(thirds, axis=1)
        sign = jnp.where(par == 1, 1.0, -1.0)
        x = lat_ref[0:1, :]
        for which in range(2):
            base = jnp.where(which == 0, par, 1 - par) * 16 + step
            for hemi in range(2):
                at = 48 * which + 24 * hemi
                r = result[at : at + 24]
                if which == 0:
                    r = r + (edge if hemi == 0 else edge * sign) * final
                slant = (x if hemi == 0 else -x) * r[6:12] - r[12:18]
                for q in range(7):
                    for c in range(2):
                        at = 2 * q + c
                        if q < 3:
                            line = r[at : at + 1]
                        elif q < 6:
                            line = slant[at - 6 : at - 5]
                        else:
                            line = r[18 + c : 19 + c]
                        rows[pl.ds(q * 32 + base + 8 * c, 1), hemi * NORTH : (hemi + 1) * NORTH] = line

    def several(step, carry):
        for j in range(UNROLL):
            one(step * UNROLL + j)
        return carry

    lax.fori_loop(0, PAIRS // UNROLL, several, 0)
    for tile in range(6):
        part = []
        for item in range(4 * tile, 4 * tile + 4):
            if item < len(ITEMS):
                q, blk = ITEMS[item]
                part.append(rows[q * 32 : (q + 1) * 32, blk * 256 : (blk + 1) * 256])
            else:
                part.append(jnp.zeros((32, 256), f32))
        turned = jnp.transpose(jnp.concatenate(part, axis=0))
        chunk_ref[:, tile * 8 : tile * 8 + 8, :] = turned.reshape(32, 8, 128)


def near(x):
    return x if INTERPRET else pltpu.with_memory_space_constraint(x, pltpu.VMEM)


def near_out(*shape):
    return jax.ShapeDtypeStruct(shape, f32) if INTERPRET else pltpu.VMEM(shape, f32)


def specs(scalars, arrays):
    return [pl.BlockSpec(memory_space=pltpu.SMEM)] * scalars + [
        pl.BlockSpec(memory_space=pltpu.VMEM)
    ] * arrays


def synthesis(place, orders, psi, temp, mag, speed, lat, norm):
    return pl.pallas_call(
        synthesis_kernel,
        in_specs=specs(2, 6),
        out_shape=jax.ShapeDtypeStruct((32, 48, 128), f32),
        scratch_shapes=[
            pltpu.VMEM((3, DEG * PAIRS, 128), f32),
            pltpu.VMEM((PAIRS, NORTH), f32),
            pltpu.VMEM((4, 24 * GROUP, 128), f32),
            pltpu.VMEM((7 * 32, NLAT), f32),
        ],
        interpret=INTERPRET,
        name="synthesis",
    )(place, orders, psi, temp, mag, speed, lat, norm)


def grid_kernel(place_ref, x_ref, below_ref, above_ref, wave_ref, order_ref, per_ref, out_ref, stage):
    inverse = 1.0 / (2.0 * (SPAN / SHELLS))
    for half in range(2):
        lanes = slice(half * 128, (half + 1) * 128)
        sources = range(half * 16, half * 16 + 16)
        for tile in range(6):
            got = block_swap([x_ref[s, tile * 8 : tile * 8 + 8, :] for s in sources], 8)
            for g in range(16):
                if tile * 4 + g // 4 >= len(ITEMS):
                    continue
                q, blk = ITEMS[tile * 4 + g // 4]
                at = q * 24 + blk * 8
                pc = g % 4
                if q in (1, 2):
                    turn = pc ^ 1
                    m = order_ref[pc // 2 : pc // 2 + 1, lanes]
                    stage[turn, at : at + 8, lanes] = got[g] * (m if pc % 2 == 0 else -m)
                else:
                    stage[pc, at : at + 8, lanes] = got[g]
        for tile in range(2):
            got = block_swap(
                [
                    (above_ref[s, tile * 8 : tile * 8 + 8, :] - below_ref[s, tile * 8 : tile * 8 + 8, :])
                    * inverse
                    for s in sources
                ],
                8,
            )
            for g in range(16):
                item = tile * 4 + g // 4
                if item < 6:
                    q, blk = ITEMS[item]
                    at = (q + 6) * 24 + blk * 8
                    stage[g % 4, at : at + 8, lanes] = got[g]
    tables = [split(wave_ref[pc]) for pc in range(4)]
    waves = []
    for pc in range(4):
        high, low = split(stage[pc])
        wave_high, wave_low = tables[pc]
        waves.append(dot_nn(high, wave_high) + (dot_nn(low, wave_high) + dot_nn(high, wave_low)))
    cos_even, sin_even, cos_odd, sin_odd = waves
    ce, se = cos_even + cos_odd, sin_even + sin_odd
    co, so = cos_even - cos_odd, sin_even - sin_odd
    images = [ce + se, ce - se, co - so, co + so]
    mine = lax.broadcasted_iota(i32, (48, 128), 1) == place_ref[0]
    both = jnp.sum(jnp.where(mine, per_ref[...], 0.0), axis=1, keepdims=True)
    radius = INNER + (SPAN / SHELLS) * (place_ref[1].astype(f32) + 0.5)
    f1 = both[0:24] / jnp.broadcast_to(radius * radius, (24, 1))
    f2 = both[24:48]
    forced = []
    for g in images:
        part = [g[q * 24 : (q + 1) * 24] for q in range(9)]
        heat = (part[3] * part[1] - part[0] * part[4]) * f1 + part[6] * part[7] * f2
        field = (part[3] * part[2] - part[0] * part[5]) * f1 + part[6] * part[8] * f2
        forced.append(jnp.concatenate([heat, field], axis=0))
    a, b = forced[0] + forced[1], forced[2] + forced[3]
    d, e = forced[0] - forced[1], forced[3] - forced[2]
    sides = [a + b, d + e, a - b, d - e]
    for par in range(2):
        parts = []
        for c in range(2):
            pc = par * 2 + c
            high, low = split(sides[pc])
            wave_high, wave_low = tables[pc]
            parts.append(dot_nt(wave_high, high) + (dot_nt(wave_high, low) + dot_nt(wave_low, high)))
        pair = jnp.concatenate(parts + [jnp.zeros((256, 32), f32)], axis=1)
        out_ref[:, par * 8 : par * 8 + 8, :] = pair.reshape(32, 8, 128)


def grid_stage(place, x, below, above, wave, order, per):
    return pl.pallas_call(
        grid_kernel,
        in_specs=specs(1, 6),
        out_shape=jax.ShapeDtypeStruct((32, 16, 128), f32),
        scratch_shapes=[pltpu.VMEM((4, 216, 256), f32)],
        interpret=INTERPRET,
        name="forcing",
    )(place, near(x), near(below), near(above), near(wave), order, per)


def analysis_kernel(
    place_ref, map_ref, v_ref, temp_ref, mag_ref, sub_ref, diag_ref, sup_ref, lat_ref, norm_ref,
    out_ref, table, last, sums, right,
):
    first = place_ref[0] * GROUP
    legendre_table(map_ref, first, lat_ref, norm_ref, table, last)

    def prepare():
        for par in range(2):
            halves = [
                block_swap(
                    [v_ref[half * 16 + s, par * 8 : par * 8 + 8, :] for s in range(16)], 8
                )
                for half in range(2)
            ]
            for c in range(2):
                for f in range(2):
                    tiles = []
                    for blk in range(3):
                        g = c * 6 + f * 3 + blk
                        tiles += [halves[0][g], halves[1][g]]
                    for eo in range(2):
                        at = par * 64 + (eo * 4 + f * 2 + c) * 8
                        for t in range(3):
                            mixed = tiles[t] + tiles[t + 3] if eo == 0 else tiles[t] - tiles[t + 3]
                            sums[t, at : at + 8, :] = mixed

    prepare()

    def one(step):
        slot_small, slot_large, small = pair_orders(map_ref, first, step)
        par = lax.rem(small, 2)

        def load(parity):
            start = parity * 64 + step
            return jnp.concatenate([sums[t, pl.ds(start, 8, stride=8), :] for t in range(3)], axis=1)

        value_small = load(par)
        high, low = split(jnp.concatenate([value_small, load(1 - par)], axis=0))
        zero = jnp.zeros((16, 128), bf16)
        halves = []
        for half in range(2):
            product = 0.0
            for t in range(3):
                cut = slice(t * 128, (t + 1) * 128)
                left = jnp.concatenate(
                    [
                        jnp.concatenate([high[:, cut], high[:, cut]], axis=1),
                        jnp.concatenate([low[:, cut], zero], axis=1),
                    ],
                    axis=0,
                )
                product = product + dot_nt(left, pair_tile(table, step, half, t))
            halves.append(product[:16] + product[16:])
        result = jnp.concatenate(halves, axis=1)
        wide = lax.broadcasted_iota(i32, (4, DEG), 1)
        picked = jnp.where(lax.rem(wide + 1 + par, 2) == 0, result[0:4], result[4:8])
        edge_value = jnp.where(par == 1, value_small[0:4], value_small[4:8])
        edge = jnp.sum(edge_value * last[pl.ds(step, 1), :], axis=1, keepdims=True)
        tendency_small = jnp.where(wide == DEG - 1, edge, roll_lanes(picked, -1))
        tendency_small = jnp.where(wide >= small, tendency_small, 0.0)
        picked = jnp.where(lax.rem(wide, 2) == 0, result[8:12], result[12:16])
        large = DEG - 1 - small
        wide8 = jnp.concatenate([picked, picked], axis=0)
        tendency_large = jnp.where(wide >= large, pltpu.roll(wide8, large, 1)[0:4], 0.0)
        for fc in range(4):
            right[fc, pl.ds(slot_small, 1), :] = tendency_small[fc : fc + 1]
            right[fc, pl.ds(slot_large, 1), :] = tendency_large[fc : fc + 1]

    def several(step, carry):
        for j in range(UNROLL):
            one(step * UNROLL + j)
        return carry

    lax.fori_loop(0, PAIRS // UNROLL, several, 0)
    for fc in range(4):
        f, c = fc // 2, fc % 2
        base = temp_ref if f == 0 else mag_ref
        right[fc, 0:GROUP, :] = base[c * GROUP : (c + 1) * GROUP, :] + STEP * right[fc, 0:GROUP, :]
        right[fc, GROUP : GROUP + 8, :] = jnp.concatenate(
            [ref[f : f + 1, :] for ref in (sub_ref, diag_ref, sup_ref)]
            + [jnp.zeros((5, DEG), f32)],
            axis=0,
        )
    for tile in range(4):
        got = block_swap([right[fc, :, tile * 128 : (tile + 1) * 128] for fc in range(4)], 32)
        for r in range(4):
            out_ref[tile * 4 + r] = got[r]


def analysis(place, orders, v, temp, mag, sub, diag, sup, lat, norm):
    return pl.pallas_call(
        analysis_kernel,
        in_specs=specs(2, 8),
        out_shape=jax.ShapeDtypeStruct((16, 24, 128), f32),
        scratch_shapes=[
            pltpu.VMEM((3, DEG * PAIRS, 128), f32),
            pltpu.VMEM((PAIRS, NORTH), f32),
            pltpu.VMEM((3, 128, 128), f32),
            pltpu.VMEM((4, GROUP + 8, DEG), f32),
        ],
        interpret=INTERPRET,
        name="analysis",
    )(place, orders, near(v), temp, mag, sub, diag, sup, lat, norm)


def solve_kernel(x_ref, out_ref):
    running = jnp.zeros((GROUP, 128), f32)
    scaled = []
    for k in range(SHELLS):
        running = x_ref[k, 0:GROUP, :] + (1.0 - x_ref[k, GROUP : GROUP + 1, :]) * running
        scaled.append(running / x_ref[k, GROUP + 1 : GROUP + 2, :])
    running = jnp.zeros((GROUP, 128), f32)
    for k in reversed(range(SHELLS)):
        running = scaled[k] + (1.0 - x_ref[k, GROUP + 2 : GROUP + 3, :]) * running
        out_ref[k] = running


def solve(x):
    return pl.pallas_call(
        solve_kernel,
        out_shape=near_out(SHELLS, GROUP, 128),
        interpret=INTERPRET,
        compiler_params=pltpu.CompilerParams(vmem_limit_bytes=8 * 2**20),
        name="radial",
    )(near(x))


def gather_kernel(x_ref, temp_ref, mag_ref):
    for tile in range(4):
        got = block_swap([x_ref[tile * 4 + r] for r in range(4)], 32)
        lanes = slice(tile * 128, (tile + 1) * 128)
        for fc in range(4):
            ref = temp_ref if fc < 2 else mag_ref
            c = fc % 2
            ref[c * GROUP : (c + 1) * GROUP, lanes] = got[fc]


def gather_stage(x):
    return pl.pallas_call(
        gather_kernel,
        out_shape=[jax.ShapeDtypeStruct((32, DEG), f32)] * 2,
        interpret=INTERPRET,
        compiler_params=pltpu.CompilerParams(vmem_limit_bytes=8 * 2**20),
        name="assemble",
    )(near(x))


def sorted_orders(orders):
    pair = orders.reshape(DEG // 2, 2)
    even = jnp.where(pair[:, 0] % 2 == 0, pair[:, 0], pair[:, 1])
    return jnp.stack([even, DEG - 1 - even])


def wave_tables(ordered):
    node = 2 * jnp.arange(QUARTER, dtype=i32) + 1
    phase = ordered[:, :, None] * node % (2 * NLON)
    angle = math.pi / NLON * phase.astype(f32)
    return jnp.stack([jnp.cos(angle), -jnp.sin(angle)], axis=1).reshape(4, DEG // 2, QUARTER)


def body(
    toroidal_stream_spectra,
    thermal_spectra,
    induction_potential,
    outward_speed_spectra,
    position_azimuth_map,
    subdiagonal_complement,
    superdiagonal_complement,
    diagonal_entries,
):
    lat, norm, per = map(jnp.asarray, host_tables())
    place = jnp.stack([lax.axis_index("ma"), lax.axis_index("row")]).astype(i32)
    psi, temp, mag, speed = (
        a.reshape(32, DEG)
        for a in (
            toroidal_stream_spectra, thermal_spectra, induction_potential, outward_speed_spectra
        )
    )
    chunk = synthesis(place, position_azimuth_map, psi, temp, mag, speed, lat, norm)
    chunk = lax.all_to_all(chunk, "ma", 0, 0, tiled=True)
    forward = [(i, i + 1) for i in range(SHELLS - 1)]
    profiles = chunk[:, 0:16, :]
    below = lax.ppermute(profiles, "row", forward)
    above = lax.ppermute(profiles, "row", [(b, a) for a, b in forward])
    ordered = sorted_orders(position_azimuth_map)
    spectra = grid_stage(
        place, chunk, below, above, wave_tables(ordered), ordered.astype(f32), per
    )
    spectra = lax.all_to_all(spectra, "ma", 0, 0, tiled=True)
    sub, diag, sup = (
        a.reshape(2, DEG) for a in (subdiagonal_complement, diagonal_entries, superdiagonal_complement)
    )
    right = analysis(
        place, position_azimuth_map, spectra, temp, mag, sub, diag, sup, lat, norm
    )
    right = lax.all_to_all(right, "row", 0, 0, tiled=True)
    solved = lax.all_to_all(solve(right), "row", 0, 0, tiled=True)
    new_temp, new_mag = gather_stage(solved)
    shape = thermal_spectra.shape
    return new_temp.reshape(shape), new_mag.reshape(shape)


def solution(mesh):
    spectra = P(None, "row", "ma", None)
    radial = P(None, "row", None)
    in_specs = (spectra,) * 4 + (P(),) + (radial,) * 3
    return jax.shard_map(
        body, mesh=mesh, in_specs=in_specs, out_specs=(spectra, spectra), check_vma=False
    )
```

```python
import math

import jax
import jax.numpy as jnp
import numpy as np
from jax import lax
from jax.experimental import pallas as pl
from jax.experimental.pallas import tpu as pltpu
from jax.sharding import PartitionSpec as P

NLAT = 768
NLON = 1536
NORTH = NLAT // 2
DEG = 512
QUARTER = NLON // 4
GROUP = 16
PAIRS = GROUP // 2
UNROLL = 4
SHELLS = 16
INNER = 0.35
SPAN = 0.65
STEP = 0.001
RENORM = 32
INTERPRET = False
ITEMS = [(q, blk) for blk in range(3) for q in (1, 2)] + [
    (q, blk) for q in (0, 3, 4, 5, 6) for blk in range(3)
]

f32 = jnp.float32
bf16 = jnp.bfloat16
i32 = jnp.int32


def host_tables():
    theta = np.pi * (np.arange(NORTH) + 0.5) / NLAT
    lat = np.zeros((8, NORTH), np.float32)
    lat[0] = np.cos(theta)
    lat[1] = np.log(np.sin(theta))
    orders = np.arange(DEG)
    log_norm = np.array(
        [
            0.5 * (math.lgamma(m + 1.5) - math.lgamma(m + 1.0) - math.lgamma(1.5))
            - 0.5 * math.log(2.0)
            for m in orders
        ]
    )
    norm = np.zeros((8, DEG), np.float32)
    norm[0] = log_norm
    k = np.arange(1, NLAT // 2 + 1)
    weights = (
        2.0
        / NLAT
        * (1.0 - 2.0 * np.sum(np.cos(2.0 * k[:, None] * theta[None]) / (4.0 * k * k - 1.0)[:, None], 0))
    )
    plain = -np.concatenate([weights, weights]) / NLON
    scaled = plain / np.concatenate([np.sin(theta), np.sin(theta)]) ** 2
    per = np.zeros((48, 128), np.float32)
    per[:, :32] = np.stack([scaled, plain]).reshape(2, 3, 32, 8).transpose(0, 1, 3, 2).reshape(48, 32)
    return lat, norm, per


def split(x):
    high = x.astype(bf16)
    return high, (x - high.astype(f32)).astype(bf16)


def dot_nn(a, b):
    return lax.dot_general(a, b, (((1,), (0,)), ((), ())), preferred_element_type=f32)


def dot_nt(a, b):
    return lax.dot_general(a, b, (((1,), (1,)), ((), ())), preferred_element_type=f32)


def roll_lanes(x, shift):
    return pltpu.roll(x, shift % x.shape[1], 1)


def block_swap(arrays, width):
    arrays = list(arrays)
    count = len(arrays)
    lane = lax.broadcasted_iota(i32, arrays[0].shape, 1) // width
    bit = 1
    while bit < count:
        low = (lane & bit) == 0
        fresh = list(arrays)
        for a in range(count):
            if a & bit == 0:
                b = a | bit
                fresh[a] = jnp.where(low, arrays[a], roll_lanes(arrays[b], bit * width))
                fresh[b] = jnp.where(low, roll_lanes(arrays[a], -bit * width), arrays[b])
        arrays = fresh
        bit *= 2
    return arrays


def pair_orders(map_ref, first, pair):
    one = map_ref[first + 2 * pair]
    two = map_ref[first + 2 * pair + 1]
    swap = (one > two).astype(i32)
    return 2 * pair + swap, 2 * pair + 1 - swap, jnp.minimum(one, two)


def legendre_table(map_ref, first, lat_ref, norm_ref, table, last):
    row8 = lax.broadcasted_iota(i32, (PAIRS, 128), 0)
    smaller = jnp.zeros((PAIRS, 128), f32)
    for i in range(PAIRS):
        smaller = jnp.where(row8 == i, pair_orders(map_ref, first, i)[2].astype(f32), smaller)
    small = smaller[:, :1]
    place = lax.broadcasted_iota(i32, (PAIRS, DEG + 128), 1).astype(f32)
    front = place <= small
    m = jnp.where(front, DEG - 1.0 - small, small)
    degree = jnp.where(front, DEG - 1.0 - small + place, place - 1.0)
    above = degree > m
    square = degree * degree - m * m
    denominator = jnp.where(above, square, 1.0)
    rise = jnp.where(
        above, jnp.sqrt(jnp.maximum(4.0 * degree * degree - 1.0, 1.0) / denominator), 0.0
    )
    lower = (degree - 1.0) * (degree - 1.0) - m * m
    fall = jnp.where(
        above,
        jnp.sqrt(
            jnp.maximum((2.0 * degree + 1.0) * lower, 0.0)
            / (jnp.maximum(2.0 * degree - 3.0, 1.0) * denominator)
        ),
        0.0,
    )
    wide = lax.broadcasted_iota(i32, (PAIRS, DEG), 1).astype(f32)

    def start(order):
        log_norm = jnp.sum(jnp.where(wide == order, norm_ref[0:1, :], 0.0), axis=1, keepdims=True)
        return log_norm + order * lat_ref[1:2, :]

    x = jnp.broadcast_to(lat_ref[0:1, :], (PAIRS, NORTH))
    log_scale = start(DEG - 1.0 - small)
    log_small = start(small)
    scale_small = jnp.exp(log_small)
    seed = small + 1.0
    before = jnp.zeros((PAIRS, NORTH), f32)
    current = jnp.ones((PAIRS, NORTH), f32)
    for tile in range(DEG // RENORM + 1):
        scale = jnp.exp(log_scale)
        for p in range(tile * RENORM, min((tile + 1) * RENORM, DEG + 1)):
            if p > 0:
                fresh = rise[:, p : p + 1] * x * current - fall[:, p : p + 1] * before
                seeded = seed == float(p)
                fresh = jnp.where(seeded, 1.0, fresh)
                scale = jnp.where(seeded, scale_small, scale)
                before, current = current, fresh
            value = current * scale
            if p < DEG:
                for t in range(3):
                    table[t, p * PAIRS : (p + 1) * PAIRS, :] = value[:, t * 128 : (t + 1) * 128]
            else:
                last[...] = value
        magnitude = jnp.maximum(jnp.abs(before), jnp.abs(current))
        magnitude = jnp.where(magnitude > 0.0, magnitude, 1.0)
        inverse_magnitude = 1.0 / magnitude
        before = before * inverse_magnitude
        current = current * inverse_magnitude
        here = (seed >= float(tile * RENORM)) & (seed < float((tile + 1) * RENORM))
        log_scale = jnp.where(here, log_small, log_scale) + jnp.log(magnitude)


def pair_tile(table, pair, half, t):
    start = half * (DEG // 2) * PAIRS + pair
    high, low = split(table[t, pl.ds(start, DEG // 2, stride=PAIRS), :])
    return jnp.concatenate([high, low], axis=1)


def synthesis_kernel(
    place_ref, map_ref, psi_ref, temp_ref, mag_ref, speed_ref, lat_ref, norm_ref,
    chunk_ref, table, last, coefs, rows,
):
    first = place_ref[0] * GROUP
    legendre_table(map_ref, first, lat_ref, norm_ref, table, last)

    def prepare():
        row16 = lax.broadcasted_iota(i32, (GROUP, 128), 0)
        natural = jnp.zeros((GROUP, 128), f32)
        for s in range(GROUP):
            natural = jnp.where(row16 == s, map_ref[first + s].astype(f32), natural)
        m = natural[:, :1]
        degree = lax.broadcasted_iota(i32, (GROUP, DEG), 1).astype(f32)
        link = jnp.where(
            degree > m,
            jnp.sqrt(
                jnp.maximum((2.0 * degree + 1.0) * (degree * degree - m * m), 0.0)
                / jnp.maximum(2.0 * degree - 1.0, 1.0)
            ),
            0.0,
        )
        weight = jnp.where(m == 0.0, 1.0, 2.0)

        def keep(at, value):
            for t in range(4):
                coefs[t, at * GROUP : (at + 1) * GROUP, :] = value[:, t * 128 : (t + 1) * 128]

        for q, ref in enumerate((psi_ref, temp_ref, mag_ref)):
            for c in range(2):
                value = ref[c * GROUP : (c + 1) * GROUP, :] * weight
                if q == 0:
                    keep(1 - c, m * value if c == 0 else -m * value)
                else:
                    keep(2 * q + c, value)
                keep(6 + 2 * q + c, value * degree)
                keep(12 + 2 * q + c, roll_lanes(value * link, -1))
        for c in range(2):
            keep(18 + c, speed_ref[c * GROUP : (c + 1) * GROUP, :] * weight)
        for at in range(20, 24):
            keep(at, jnp.zeros((GROUP, DEG), f32))

    prepare()

    def one(step):
        final = last[pl.ds(step, 1), :]

        slot_small, slot_large, small = pair_orders(map_ref, first, step)
        par = lax.rem(small, 2)
        wide = lax.broadcasted_iota(i32, (24, DEG), 1)

        def load(slot):
            return jnp.concatenate(
                [coefs[t, pl.ds(slot, 24, stride=GROUP), :] for t in range(4)], axis=1
            )

        plain = load(slot_small)
        edge = plain[:, DEG - 1 :]
        north = jnp.where(wide == 0, 0.0, roll_lanes(plain, 1))
        flip = lax.rem(wide + 1 + par, 2) == 0
        south = jnp.where(flip, north, -north)
        north_large = pltpu.roll(load(slot_large), small + 1, 1)
        south_large = jnp.where(lax.rem(wide, 2) == 0, north_large, -north_large)
        high, low = split(jnp.concatenate([north, south, north_large, south_large], axis=0))
        both = jnp.concatenate([high, low], axis=0)
        thirds = []
        for t in range(3):
            product = dot_nn(both[:, : DEG // 2], pair_tile(table, step, 0, t)) + dot_nn(
                both[:, DEG // 2 :], pair_tile(table, step, 1, t)
            )
            thirds.append(product[:96, :128] + (product[96:, :128] + product[:96, 128:]))
        result = jnp.concatenate(thirds, axis=1)
        sign = jnp.where(par == 1, 1.0, -1.0)
        x = lat_ref[0:1, :]
        for which in range(2):
            base = jnp.where(which == 0, par, 1 - par) * 16 + step
            for hemi in range(2):
                at = 48 * which + 24 * hemi
                r = result[at : at + 24]
                if which == 0:
                    r = r + (edge if hemi == 0 else edge * sign) * final
                slant = (x if hemi == 0 else -x) * r[6:12] - r[12:18]
                for q in range(7):
                    for c in range(2):
                        at = 2 * q + c
                        if q < 3:
                            line = r[at : at + 1]
                        elif q < 6:
                            line = slant[at - 6 : at - 5]
                        else:
                            line = r[18 + c : 19 + c]
                        rows[pl.ds(q * 32 + base + 8 * c, 1), hemi * NORTH : (hemi + 1) * NORTH] = line

    def several(step, carry):
        for j in range(UNROLL):
            one(step * UNROLL + j)
        return carry

    lax.fori_loop(0, PAIRS // UNROLL, several, 0)
    for tile in range(6):
        part = []
        for item in range(4 * tile, 4 * tile + 4):
            if item < len(ITEMS):
                q, blk = ITEMS[item]
                part.append(rows[q * 32 : (q + 1) * 32, blk * 256 : (blk + 1) * 256])
            else:
                part.append(jnp.zeros((32, 256), f32))
        turned = jnp.transpose(jnp.concatenate(part, axis=0))
        chunk_ref[:, tile * 8 : tile * 8 + 8, :] = turned.reshape(32, 8, 128)


def near(x):
    return x if INTERPRET else pltpu.with_memory_space_constraint(x, pltpu.VMEM)


def near_out(*shape):
    return jax.ShapeDtypeStruct(shape, f32) if INTERPRET else pltpu.VMEM(shape, f32)


def specs(scalars, arrays):
    return [pl.BlockSpec(memory_space=pltpu.SMEM)] * scalars + [
        pl.BlockSpec(memory_space=pltpu.VMEM)
    ] * arrays


def synthesis(place, orders, psi, temp, mag, speed, lat, norm):
    return pl.pallas_call(
        synthesis_kernel,
        in_specs=specs(2, 6),
        out_shape=near_out(32, 48, 128),
        scratch_shapes=[
            pltpu.VMEM((3, DEG * PAIRS, 128), f32),
            pltpu.VMEM((PAIRS, NORTH), f32),
            pltpu.VMEM((4, 24 * GROUP, 128), f32),
            pltpu.VMEM((7 * 32, NLAT), f32),
        ],
        interpret=INTERPRET,
        name="synthesis",
    )(place, orders, psi, temp, mag, speed, lat, norm)


def spread(tables, stage, rows):
    waves = []
    for pc in range(4):
        high, low = split(stage[pc, 0:rows, :])
        wave_high, wave_low = tables[pc]
        waves.append(dot_nn(high, wave_high) + (dot_nn(low, wave_high) + dot_nn(high, wave_low)))
    cos_even, sin_even, cos_odd, sin_odd = waves
    ce, se = cos_even + cos_odd, sin_even + sin_odd
    co, so = cos_even - cos_odd, sin_even - sin_odd
    return [ce + se, ce - se, co - so, co + so]


def flow_kernel(place_ref, shell_ref, x_ref, wave_ref, order_ref, per_ref, out_ref, stage):
    for half in range(2):
        lanes = slice(half * 128, (half + 1) * 128)
        for tile in range(6):
            got = block_swap(
                [x_ref[s, tile * 8 : tile * 8 + 8, :] for s in range(half * 16, half * 16 + 16)], 8
            )
            for g in range(16):
                if tile * 4 + g // 4 >= len(ITEMS):
                    continue
                q, blk = ITEMS[tile * 4 + g // 4]
                at = q * 24 + blk * 8
                pc = g % 4
                if q in (1, 2):
                    turn = pc ^ 1
                    m = order_ref[pc // 2 : pc // 2 + 1, lanes]
                    stage[turn, at : at + 8, lanes] = got[g] * (m if pc % 2 == 0 else -m)
                else:
                    stage[pc, at : at + 8, lanes] = got[g]
    tables = [split(wave_ref[pc]) for pc in range(4)]
    images = spread(tables, stage, 7 * 24)
    mine = lax.broadcasted_iota(i32, (48, 128), 1) == place_ref[0]
    both = jnp.sum(jnp.where(mine, per_ref[...], 0.0), axis=1, keepdims=True)
    radius = INNER + (SPAN / SHELLS) * (shell_ref[0].astype(f32) + 0.5)
    f1 = both[0:24] / jnp.broadcast_to(radius * radius, (24, 1))
    f2 = both[24:48]
    for n, g in enumerate(images):
        part = [g[q * 24 : (q + 1) * 24] for q in range(7)]
        out_ref[n, 0:24, :] = (part[3] * part[1] - part[0] * part[4]) * f1
        out_ref[n, 24:48, :] = (part[3] * part[2] - part[0] * part[5]) * f1
        out_ref[n, 48:72, :] = part[6] * f2


def flow_stage(place, shell, x, wave, order, per):
    return pl.pallas_call(
        flow_kernel,
        in_specs=specs(2, 4),
        out_shape=near_out(4, 72, QUARTER),
        scratch_shapes=[pltpu.VMEM((4, 7 * 24, 256), f32)],
        interpret=INTERPRET,
        compiler_params=pltpu.CompilerParams(vmem_limit_bytes=24 * 2**20),
        name="flow",
    )(place, shell, near(x), near(wave), order, per)


def forcing_kernel(shell_ref, chip_ref, link_ref, wave_ref, flow_ref, out_ref, stage):
    even = lax.rem(shell_ref[0], 2) == 0
    inverse = jnp.where(even, 1.0, -1.0) / (2.0 * (SPAN / SHELLS))
    for half in range(2):
        lanes = slice(half * 128, (half + 1) * 128)
        for tile in range(2):
            rows = slice(tile * 8, tile * 8 + 8)
            got = block_swap(
                [
                    (chip_ref[s, rows, :] - link_ref[s, rows, :]) * inverse
                    for s in range(half * 16, half * 16 + 16)
                ],
                8,
            )
            for g in range(16):
                item = tile * 4 + g // 4
                if item < 6:
                    q, blk = ITEMS[item]
                    at = (q - 1) * 24 + blk * 8
                    stage[g % 4, at : at + 8, lanes] = got[g]
    tables = [split(wave_ref[pc]) for pc in range(4)]
    forced = []
    for n, g in enumerate(spread(tables, stage, 48)):
        speed = flow_ref[n, 48:72, :]
        heat = flow_ref[n, 0:24, :] + speed * g[0:24]
        field = flow_ref[n, 24:48, :] + speed * g[24:48]
        forced.append(jnp.concatenate([heat, field], axis=0))
    a, b = forced[0] + forced[1], forced[2] + forced[3]
    d, e = forced[0] - forced[1], forced[3] - forced[2]
    sides = [a + b, d + e, a - b, d - e]
    for par in range(2):
        parts = []
        for c in range(2):
            pc = par * 2 + c
            high, low = split(sides[pc])
            wave_high, wave_low = tables[pc]
            parts.append(dot_nt(wave_high, high) + (dot_nt(wave_high, low) + dot_nt(wave_low, high)))
        pair = jnp.concatenate(parts + [jnp.zeros((256, 32), f32)], axis=1)
        out_ref[:, par * 8 : par * 8 + 8, :] = pair.reshape(32, 8, 128)


def forcing_stage(shell, chip, link, wave, flow):
    return pl.pallas_call(
        forcing_kernel,
        in_specs=specs(1, 4),
        out_shape=near_out(32, 16, 128),
        scratch_shapes=[pltpu.VMEM((4, 48, 256), f32)],
        interpret=INTERPRET,
        compiler_params=pltpu.CompilerParams(vmem_limit_bytes=24 * 2**20),
        name="forcing",
    )(shell, near(chip), near(link), near(wave), near(flow))


def table_kernel(place_ref, map_ref, lat_ref, norm_ref, after_ref, tab_ref, last, table, ready, sems):
    legendre_table(map_ref, place_ref[0] * GROUP, lat_ref, norm_ref, table, last)
    copies = []
    for pair in range(PAIRS):
        for half in range(2):
            rows = slice(half * (DEG // 2), (half + 1) * (DEG // 2))
            for t in range(3):
                start = half * (DEG // 2) * PAIRS + pair
                turned = jnp.transpose(table[t, pl.ds(start, DEG // 2, stride=PAIRS), :])
                high, low = split(turned)
                ready[pair, t * 256 : t * 256 + 128, rows] = high
                ready[pair, t * 256 + 128 : (t + 1) * 256, rows] = low
        copy = pltpu.make_async_copy(ready.at[pair], tab_ref.at[pair], sems.at[pair])
        copy.start()
        copies.append(copy)
    for copy in copies:
        copy.wait()


def tables(place, orders, lat, norm, after):
    return pl.pallas_call(
        table_kernel,
        in_specs=specs(2, 2) + [pl.BlockSpec(memory_space=pl.ANY)],
        out_specs=[pl.BlockSpec(memory_space=pl.ANY), pl.BlockSpec(memory_space=pltpu.VMEM)],
        out_shape=[
            jax.ShapeDtypeStruct((PAIRS, 2 * NORTH, DEG), bf16),
            jax.ShapeDtypeStruct((PAIRS, NORTH), f32),
        ],
        scratch_shapes=[
            pltpu.VMEM((3, DEG * PAIRS, 128), f32),
            pltpu.VMEM((PAIRS, 2 * NORTH, DEG), bf16),
            pltpu.SemaphoreType.DMA((PAIRS,)),
        ],
        interpret=INTERPRET,
        name="legendre",
    )(place, orders, lat, norm, after)


def analysis_kernel(
    place_ref, map_ref, v_ref, temp_ref, mag_ref, sub_ref, diag_ref, sup_ref, last, tab_ref,
    out_ref, ready, sums, right, sems,
):
    first = place_ref[0] * GROUP
    copies = [
        pltpu.make_async_copy(tab_ref.at[pair], ready.at[pair], sems.at[pair]) for pair in range(PAIRS)
    ]
    for copy in copies:
        copy.start()

    def prepare():
        for par in range(2):
            halves = [
                block_swap(
                    [v_ref[half * 16 + s, par * 8 : par * 8 + 8, :] for s in range(16)], 8
                )
                for half in range(2)
            ]
            for c in range(2):
                for f in range(2):
                    tiles = []
                    for blk in range(3):
                        g = c * 6 + f * 3 + blk
                        tiles += [halves[0][g], halves[1][g]]
                    for eo in range(2):
                        at = par * 64 + (eo * 4 + f * 2 + c) * 8
                        for t in range(3):
                            mixed = tiles[t] + tiles[t + 3] if eo == 0 else tiles[t] - tiles[t + 3]
                            sums[t, at : at + 8, :] = mixed

    prepare()

    def one(step):
        slot_small, slot_large, small = pair_orders(map_ref, first, step)
        par = lax.rem(small, 2)

        def load(parity):
            start = parity * 64 + step
            return jnp.concatenate([sums[t, pl.ds(start, 8, stride=8), :] for t in range(3)], axis=1)

        value_small = load(par)
        high, low = split(jnp.concatenate([value_small, load(1 - par)], axis=0))
        zero = jnp.zeros((16, 128), bf16)
        halves = []
        for half in range(2):
            product = 0.0
            for t in range(3):
                cut = slice(t * 128, (t + 1) * 128)
                left = jnp.concatenate(
                    [
                        jnp.concatenate([high[:, cut], high[:, cut]], axis=1),
                        jnp.concatenate([low[:, cut], zero], axis=1),
                    ],
                    axis=0,
                )
                rows = slice(half * (DEG // 2), (half + 1) * (DEG // 2))
                product = product + dot_nn(left, ready[step, t * 256 : (t + 1) * 256, rows])
            halves.append(product[:16] + product[16:])
        result = jnp.concatenate(halves, axis=1)
        wide = lax.broadcasted_iota(i32, (4, DEG), 1)
        picked = jnp.where(lax.rem(wide + 1 + par, 2) == 0, result[0:4], result[4:8])
        edge_value = jnp.where(par == 1, value_small[0:4], value_small[4:8])
        edge = jnp.sum(edge_value * last[pl.ds(step, 1), :], axis=1, keepdims=True)
        tendency_small = jnp.where(wide == DEG - 1, edge, roll_lanes(picked, -1))
        tendency_small = jnp.where(wide >= small, tendency_small, 0.0)
        picked = jnp.where(lax.rem(wide, 2) == 0, result[8:12], result[12:16])
        large = DEG - 1 - small
        wide8 = jnp.concatenate([picked, picked], axis=0)
        tendency_large = jnp.where(wide >= large, pltpu.roll(wide8, large, 1)[0:4], 0.0)
        for fc in range(4):
            right[fc, pl.ds(slot_small, 1), :] = tendency_small[fc : fc + 1]
            right[fc, pl.ds(slot_large, 1), :] = tendency_large[fc : fc + 1]

    for pair in range(PAIRS):
        copies[pair].wait()
        one(pair)
    for fc in range(4):
        f, c = fc // 2, fc % 2
        base = temp_ref if f == 0 else mag_ref
        right[fc, 0:GROUP, :] = base[c * GROUP : (c + 1) * GROUP, :] + STEP * right[fc, 0:GROUP, :]
        right[fc, GROUP : GROUP + 8, :] = jnp.concatenate(
            [ref[f : f + 1, :] for ref in (sub_ref, diag_ref, sup_ref)]
            + [jnp.zeros((5, DEG), f32)],
            axis=0,
        )
    for tile in range(4):
        got = block_swap([right[fc, :, tile * 128 : (tile + 1) * 128] for fc in range(4)], 32)
        for r in range(4):
            out_ref[tile * 4 + r] = got[r]


def analysis(place, orders, v, temp, mag, sub, diag, sup, last, tab):
    return pl.pallas_call(
        analysis_kernel,
        in_specs=specs(2, 7) + [pl.BlockSpec(memory_space=pl.ANY)],
        out_shape=near_out(16, 24, 128),
        scratch_shapes=[
            pltpu.VMEM((PAIRS, 2 * NORTH, DEG), bf16),
            pltpu.VMEM((3, 128, 128), f32),
            pltpu.VMEM((4, GROUP + 8, DEG), f32),
            pltpu.SemaphoreType.DMA((PAIRS,)),
        ],
        interpret=INTERPRET,
        name="analysis",
    )(place, orders, near(v), temp, mag, sub, diag, sup, last, tab)


def solve_kernel(x_ref, out_ref):
    running = jnp.zeros((GROUP, 128), f32)
    scaled = []
    for k in range(SHELLS):
        running = x_ref[k, 0:GROUP, :] + (1.0 - x_ref[k, GROUP : GROUP + 1, :]) * running
        scaled.append(running / x_ref[k, GROUP + 1 : GROUP + 2, :])
    running = jnp.zeros((GROUP, 128), f32)
    for k in reversed(range(SHELLS)):
        running = scaled[k] + (1.0 - x_ref[k, GROUP + 2 : GROUP + 3, :]) * running
        out_ref[k] = running


def solve(x):
    return pl.pallas_call(
        solve_kernel,
        out_shape=near_out(SHELLS, GROUP, 128),
        interpret=INTERPRET,
        compiler_params=pltpu.CompilerParams(vmem_limit_bytes=8 * 2**20),
        name="radial",
    )(near(x))


def gather_kernel(x_ref, temp_ref, mag_ref):
    for tile in range(4):
        got = block_swap([x_ref[tile * 4 + r] for r in range(4)], 32)
        lanes = slice(tile * 128, (tile + 1) * 128)
        for fc in range(4):
            ref = temp_ref if fc < 2 else mag_ref
            c = fc % 2
            ref[c * GROUP : (c + 1) * GROUP, lanes] = got[fc]


def gather_stage(x):
    return pl.pallas_call(
        gather_kernel,
        out_shape=[jax.ShapeDtypeStruct((32, DEG), f32)] * 2,
        interpret=INTERPRET,
        compiler_params=pltpu.CompilerParams(vmem_limit_bytes=8 * 2**20),
        name="assemble",
    )(near(x))


def sorted_orders(orders):
    pair = orders.reshape(DEG // 2, 2)
    even = jnp.where(pair[:, 0] % 2 == 0, pair[:, 0], pair[:, 1])
    return jnp.stack([even, DEG - 1 - even])


def wave_tables(ordered):
    node = 2 * jnp.arange(QUARTER, dtype=i32) + 1
    phase = ordered[:, :, None] * node % (2 * NLON)
    angle = math.pi / NLON * phase.astype(f32)
    return jnp.stack([jnp.cos(angle), -jnp.sin(angle)], axis=1).reshape(4, DEG // 2, QUARTER)


def body(
    toroidal_stream_spectra,
    thermal_spectra,
    induction_potential,
    outward_speed_spectra,
    position_azimuth_map,
    subdiagonal_complement,
    superdiagonal_complement,
    diagonal_entries,
):
    lat, norm, per = map(jnp.asarray, host_tables())
    place = lax.axis_index("ma").reshape(1).astype(i32)
    shell = lax.axis_index("row").reshape(1).astype(i32)
    psi, temp, mag, speed = (
        a.reshape(32, DEG)
        for a in (
            toroidal_stream_spectra, thermal_spectra, induction_potential, outward_speed_spectra
        )
    )
    chunk = synthesis(place, position_azimuth_map, psi, temp, mag, speed, lat, norm)
    tab, last = tables(place, position_azimuth_map, lat, norm, chunk)
    chunk = lax.all_to_all(chunk, "ma", 0, 0, tiled=True)
    ordered = sorted_orders(position_azimuth_map)
    wave = wave_tables(ordered)
    chunk, wave, tab, last = lax.optimization_barrier((chunk, wave, tab, last))
    profiles = chunk[:, 0:16, :]
    near_pairs = [(i, i ^ 1) for i in range(SHELLS)]
    far_pairs = [(i, i + 1) for i in range(1, SHELLS - 1, 2)]
    far_pairs += [(b, a) for a, b in far_pairs]
    link = lax.ppermute(profiles, "row", far_pairs)
    chip = lax.ppermute(profiles, "row", near_pairs)
    flow = flow_stage(place, shell, chunk, wave, ordered.astype(f32), per)
    spectra = forcing_stage(shell, chip, link, wave, flow)
    spectra = lax.all_to_all(spectra, "ma", 0, 0, tiled=True)
    sub, diag, sup = (
        a.reshape(2, DEG) for a in (subdiagonal_complement, diagonal_entries, superdiagonal_complement)
    )
    right = analysis(
        place, position_azimuth_map, spectra, temp, mag, sub, diag, sup, last, tab
    )
    right = lax.all_to_all(right, "row", 0, 0, tiled=True)
    solved = lax.all_to_all(solve(right), "row", 0, 0, tiled=True)
    new_temp, new_mag = gather_stage(solved)
    shape = thermal_spectra.shape
    return new_temp.reshape(shape), new_mag.reshape(shape)


def solution(mesh):
    spectra = P(None, "row", "ma", None)
    radial = P(None, "row", None)
    in_specs = (spectra,) * 4 + (P(),) + (radial,) * 3
    return jax.shard_map(
        body, mesh=mesh, in_specs=in_specs, out_specs=(spectra, spectra), check_vma=False
    )
```

```python
import math

import jax
import jax.numpy as jnp
import numpy as np
from jax import lax
from jax.experimental import pallas as pl
from jax.experimental.pallas import tpu as pltpu
from jax.sharding import PartitionSpec as P

NLAT = 768
NLON = 1536
NORTH = NLAT // 2
DEG = 512
QUARTER = NLON // 4
GROUP = 16
PAIRS = GROUP // 2
UNROLL = 8
SHELLS = 16
INNER = 0.35
SPAN = 0.65
STEP = 0.001
RENORM = 32
INTERPRET = False
ITEMS = [(q, blk) for blk in range(3) for q in (1, 2)] + [
    (q, blk) for q in (0, 3, 4, 5, 6) for blk in range(3)
]

f32 = jnp.float32
bf16 = jnp.bfloat16
i32 = jnp.int32


def host_tables():
    theta = np.pi * (np.arange(NORTH) + 0.5) / NLAT
    lat = np.zeros((8, NORTH), np.float32)
    lat[0] = np.cos(theta)
    lat[1] = np.log(np.sin(theta))
    orders = np.arange(DEG)
    log_norm = np.array(
        [
            0.5 * (math.lgamma(m + 1.5) - math.lgamma(m + 1.0) - math.lgamma(1.5))
            - 0.5 * math.log(2.0)
            for m in orders
        ]
    )
    norm = np.zeros((8, DEG), np.float32)
    norm[0] = log_norm
    k = np.arange(1, NLAT // 2 + 1)
    weights = (
        2.0
        / NLAT
        * (1.0 - 2.0 * np.sum(np.cos(2.0 * k[:, None] * theta[None]) / (4.0 * k * k - 1.0)[:, None], 0))
    )
    plain = -np.concatenate([weights, weights]) / NLON
    scaled = plain / np.concatenate([np.sin(theta), np.sin(theta)]) ** 2
    per = np.zeros((48, 128), np.float32)
    per[:, :32] = np.stack([scaled, plain]).reshape(2, 3, 32, 8).transpose(0, 1, 3, 2).reshape(48, 32)
    return lat, norm, per


def split(x):
    high = x.astype(bf16)
    return high, (x - high.astype(f32)).astype(bf16)


def dot_nn(a, b):
    return lax.dot_general(a, b, (((1,), (0,)), ((), ())), preferred_element_type=f32)


def dot_nt(a, b):
    return lax.dot_general(a, b, (((1,), (1,)), ((), ())), preferred_element_type=f32)


def roll_lanes(x, shift):
    return pltpu.roll(x, shift % x.shape[1], 1)


def block_swap(arrays, width):
    arrays = list(arrays)
    count = len(arrays)
    lane = lax.broadcasted_iota(i32, arrays[0].shape, 1) // width
    bit = 1
    while bit < count:
        low = (lane & bit) == 0
        fresh = list(arrays)
        for a in range(count):
            if a & bit == 0:
                b = a | bit
                fresh[a] = jnp.where(low, arrays[a], roll_lanes(arrays[b], bit * width))
                fresh[b] = jnp.where(low, roll_lanes(arrays[a], -bit * width), arrays[b])
        arrays = fresh
        bit *= 2
    return arrays


def pair_orders(map_ref, first, pair):
    one = map_ref[first + 2 * pair]
    two = map_ref[first + 2 * pair + 1]
    swap = (one > two).astype(i32)
    return 2 * pair + swap, 2 * pair + 1 - swap, jnp.minimum(one, two)


def legendre_table(map_ref, first, lat_ref, norm_ref, table, last):
    row8 = lax.broadcasted_iota(i32, (PAIRS, 128), 0)
    smaller = jnp.zeros((PAIRS, 128), f32)
    for i in range(PAIRS):
        smaller = jnp.where(row8 == i, pair_orders(map_ref, first, i)[2].astype(f32), smaller)
    small = smaller[:, :1]
    place = lax.broadcasted_iota(i32, (PAIRS, DEG + 128), 1).astype(f32)
    front = place <= small
    m = jnp.where(front, DEG - 1.0 - small, small)
    degree = jnp.where(front, DEG - 1.0 - small + place, place - 1.0)
    above = degree > m
    square = degree * degree - m * m
    denominator = jnp.where(above, square, 1.0)
    rise = jnp.where(
        above, jnp.sqrt(jnp.maximum(4.0 * degree * degree - 1.0, 1.0) / denominator), 0.0
    )
    lower = (degree - 1.0) * (degree - 1.0) - m * m
    fall = jnp.where(
        above,
        jnp.sqrt(
            jnp.maximum((2.0 * degree + 1.0) * lower, 0.0)
            / (jnp.maximum(2.0 * degree - 3.0, 1.0) * denominator)
        ),
        0.0,
    )
    wide = lax.broadcasted_iota(i32, (PAIRS, DEG), 1).astype(f32)

    def start(order):
        log_norm = jnp.sum(jnp.where(wide == order, norm_ref[0:1, :], 0.0), axis=1, keepdims=True)
        return log_norm + order * lat_ref[1:2, :]

    x = jnp.broadcast_to(lat_ref[0:1, :], (PAIRS, NORTH))
    log_scale = start(DEG - 1.0 - small)
    log_small = start(small)
    scale_small = jnp.exp(log_small)
    seed = small + 1.0
    before = jnp.zeros((PAIRS, NORTH), f32)
    current = jnp.ones((PAIRS, NORTH), f32)
    for tile in range(DEG // RENORM + 1):
        scale = jnp.exp(log_scale)
        for p in range(tile * RENORM, min((tile + 1) * RENORM, DEG + 1)):
            if p > 0:
                fresh = rise[:, p : p + 1] * x * current - fall[:, p : p + 1] * before
                seeded = seed == float(p)
                fresh = jnp.where(seeded, 1.0, fresh)
                scale = jnp.where(seeded, scale_small, scale)
                before, current = current, fresh
            value = current * scale
            if p < DEG:
                for t in range(3):
                    table[t, p * PAIRS : (p + 1) * PAIRS, :] = value[:, t * 128 : (t + 1) * 128]
            else:
                last[...] = value
        magnitude = jnp.maximum(jnp.abs(before), jnp.abs(current))
        magnitude = jnp.where(magnitude > 0.0, magnitude, 1.0)
        inverse_magnitude = 1.0 / magnitude
        before = before * inverse_magnitude
        current = current * inverse_magnitude
        here = (seed >= float(tile * RENORM)) & (seed < float((tile + 1) * RENORM))
        log_scale = jnp.where(here, log_small, log_scale) + jnp.log(magnitude)


def pair_tile(table, pair, half, t):
    start = half * (DEG // 2) * PAIRS + pair
    high, low = split(table[t, pl.ds(start, DEG // 2, stride=PAIRS), :])
    return jnp.concatenate([high, low], axis=1)


def synthesis_kernel(
    place_ref, map_ref, psi_ref, temp_ref, mag_ref, speed_ref, lat_ref, norm_ref,
    chunk_ref, table, last, coefs, rows,
):
    first = place_ref[0] * GROUP
    legendre_table(map_ref, first, lat_ref, norm_ref, table, last)

    def prepare():
        row16 = lax.broadcasted_iota(i32, (GROUP, 128), 0)
        natural = jnp.zeros((GROUP, 128), f32)
        for s in range(GROUP):
            natural = jnp.where(row16 == s, map_ref[first + s].astype(f32), natural)
        m = natural[:, :1]
        degree = lax.broadcasted_iota(i32, (GROUP, DEG), 1).astype(f32)
        link = jnp.where(
            degree > m,
            jnp.sqrt(
                jnp.maximum((2.0 * degree + 1.0) * (degree * degree - m * m), 0.0)
                / jnp.maximum(2.0 * degree - 1.0, 1.0)
            ),
            0.0,
        )
        weight = jnp.where(m == 0.0, 1.0, 2.0)

        def keep(at, value):
            for t in range(4):
                coefs[t, at * GROUP : (at + 1) * GROUP, :] = value[:, t * 128 : (t + 1) * 128]

        for q, ref in enumerate((psi_ref, temp_ref, mag_ref)):
            for c in range(2):
                value = ref[c * GROUP : (c + 1) * GROUP, :] * weight
                if q == 0:
                    keep(1 - c, m * value if c == 0 else -m * value)
                else:
                    keep(2 * q + c, value)
                keep(6 + 2 * q + c, value * degree)
                keep(12 + 2 * q + c, roll_lanes(value * link, -1))
        for c in range(2):
            keep(18 + c, speed_ref[c * GROUP : (c + 1) * GROUP, :] * weight)
        for at in range(20, 24):
            keep(at, jnp.zeros((GROUP, DEG), f32))

    prepare()

    def one(step):
        final = last[pl.ds(step, 1), :]

        slot_small, slot_large, small = pair_orders(map_ref, first, step)
        par = lax.rem(small, 2)
        wide = lax.broadcasted_iota(i32, (24, DEG), 1)

        def load(slot):
            return jnp.concatenate(
                [coefs[t, pl.ds(slot, 24, stride=GROUP), :] for t in range(4)], axis=1
            )

        plain = load(slot_small)
        edge = plain[:, DEG - 1 :]
        north = jnp.where(wide == 0, 0.0, roll_lanes(plain, 1))
        flip = lax.rem(wide + 1 + par, 2) == 0
        south = jnp.where(flip, north, -north)
        north_large = pltpu.roll(load(slot_large), small + 1, 1)
        south_large = jnp.where(lax.rem(wide, 2) == 0, north_large, -north_large)
        high, low = split(jnp.concatenate([north, south, north_large, south_large], axis=0))
        both = jnp.concatenate([high, low], axis=0)
        thirds = []
        for t in range(3):
            product = dot_nn(both[:, : DEG // 2], pair_tile(table, step, 0, t)) + dot_nn(
                both[:, DEG // 2 :], pair_tile(table, step, 1, t)
            )
            thirds.append(product[:96, :128] + (product[96:, :128] + product[:96, 128:]))
        result = jnp.concatenate(thirds, axis=1)
        sign = jnp.where(par == 1, 1.0, -1.0)
        x = lat_ref[0:1, :]
        for which in range(2):
            base = jnp.where(which == 0, par, 1 - par) * 16 + step
            for hemi in range(2):
                at = 48 * which + 24 * hemi
                r = result[at : at + 24]
                if which == 0:
                    r = r + (edge if hemi == 0 else edge * sign) * final
                slant = (x if hemi == 0 else -x) * r[6:12] - r[12:18]
                for q in range(7):
                    for c in range(2):
                        at = 2 * q + c
                        if q < 3:
                            line = r[at : at + 1]
                        elif q < 6:
                            line = slant[at - 6 : at - 5]
                        else:
                            line = r[18 + c : 19 + c]
                        rows[pl.ds(q * 32 + base + 8 * c, 1), hemi * NORTH : (hemi + 1) * NORTH] = line

    def several(step, carry):
        for j in range(UNROLL):
            one(step * UNROLL + j)
        return carry

    lax.fori_loop(0, PAIRS // UNROLL, several, 0)
    for tile in range(6):
        part = []
        for item in range(4 * tile, 4 * tile + 4):
            if item < len(ITEMS):
                q, blk = ITEMS[item]
                part.append(rows[q * 32 : (q + 1) * 32, blk * 256 : (blk + 1) * 256])
            else:
                part.append(jnp.zeros((32, 256), f32))
        turned = jnp.transpose(jnp.concatenate(part, axis=0))
        chunk_ref[:, tile * 8 : tile * 8 + 8, :] = turned.reshape(32, 8, 128)


def near(x):
    return x if INTERPRET else pltpu.with_memory_space_constraint(x, pltpu.VMEM)


def near_out(*shape):
    return jax.ShapeDtypeStruct(shape, f32) if INTERPRET else pltpu.VMEM(shape, f32)


def specs(scalars, arrays):
    return [pl.BlockSpec(memory_space=pltpu.SMEM)] * scalars + [
        pl.BlockSpec(memory_space=pltpu.VMEM)
    ] * arrays


def synthesis(place, orders, psi, temp, mag, speed, lat, norm):
    return pl.pallas_call(
        synthesis_kernel,
        in_specs=specs(2, 6),
        out_shape=near_out(32, 48, 128),
        scratch_shapes=[
            pltpu.VMEM((3, DEG * PAIRS, 128), f32),
            pltpu.VMEM((PAIRS, NORTH), f32),
            pltpu.VMEM((4, 24 * GROUP, 128), f32),
            pltpu.VMEM((7 * 32, NLAT), f32),
        ],
        interpret=INTERPRET,
        name="synthesis",
    )(place, orders, psi, temp, mag, speed, lat, norm)


def spread(tables, stage, rows):
    waves = []
    for pc in range(4):
        high, low = split(stage[pc, 0:rows, :])
        wave_high, wave_low = tables[pc]
        both = dot_nn(jnp.concatenate([high, low], axis=0), wave_high)
        waves.append(both[:rows] + (both[rows:] + dot_nn(high, wave_low)))
    cos_even, sin_even, cos_odd, sin_odd = waves
    ce, se = cos_even + cos_odd, sin_even + sin_odd
    co, so = cos_even - cos_odd, sin_even - sin_odd
    return [ce + se, ce - se, co - so, co + so]


def flow_kernel(place_ref, shell_ref, x_ref, wave_ref, order_ref, per_ref, out_ref, stage):
    for half in range(2):
        lanes = slice(half * 128, (half + 1) * 128)
        for tile in range(6):
            got = block_swap(
                [x_ref[s, tile * 8 : tile * 8 + 8, :] for s in range(half * 16, half * 16 + 16)], 8
            )
            for g in range(16):
                if tile * 4 + g // 4 >= len(ITEMS):
                    continue
                q, blk = ITEMS[tile * 4 + g // 4]
                at = q * 24 + blk * 8
                pc = g % 4
                if q in (1, 2):
                    turn = pc ^ 1
                    m = order_ref[pc // 2 : pc // 2 + 1, lanes]
                    stage[turn, at : at + 8, lanes] = got[g] * (m if pc % 2 == 0 else -m)
                else:
                    stage[pc, at : at + 8, lanes] = got[g]
    tables = [split(wave_ref[pc]) for pc in range(4)]
    images = spread(tables, stage, 7 * 24)
    mine = lax.broadcasted_iota(i32, (48, 128), 1) == place_ref[0]
    both = jnp.sum(jnp.where(mine, per_ref[...], 0.0), axis=1, keepdims=True)
    radius = INNER + (SPAN / SHELLS) * (shell_ref[0].astype(f32) + 0.5)
    f1 = both[0:24] / jnp.broadcast_to(radius * radius, (24, 1))
    f2 = both[24:48]
    for n, g in enumerate(images):
        part = [g[q * 24 : (q + 1) * 24] for q in range(7)]
        out_ref[n, 0:24, :] = (part[3] * part[1] - part[0] * part[4]) * f1
        out_ref[n, 24:48, :] = (part[3] * part[2] - part[0] * part[5]) * f1
        out_ref[n, 48:72, :] = part[6] * f2


def flow_stage(place, shell, x, wave, order, per):
    return pl.pallas_call(
        flow_kernel,
        in_specs=specs(2, 4),
        out_shape=near_out(4, 72, QUARTER),
        scratch_shapes=[pltpu.VMEM((4, 7 * 24, 256), f32)],
        interpret=INTERPRET,
        compiler_params=pltpu.CompilerParams(vmem_limit_bytes=24 * 2**20),
        name="flow",
    )(place, shell, near(x), near(wave), order, per)


def forcing_kernel(shell_ref, chip_ref, link_ref, wave_ref, flow_ref, out_ref, stage):
    even = lax.rem(shell_ref[0], 2) == 0
    inverse = jnp.where(even, 1.0, -1.0) / (2.0 * (SPAN / SHELLS))
    for half in range(2):
        lanes = slice(half * 128, (half + 1) * 128)
        for tile in range(2):
            rows = slice(tile * 8, tile * 8 + 8)
            got = block_swap(
                [
                    (chip_ref[s, rows, :] - link_ref[s, rows, :]) * inverse
                    for s in range(half * 16, half * 16 + 16)
                ],
                8,
            )
            for g in range(16):
                item = tile * 4 + g // 4
                if item < 6:
                    q, blk = ITEMS[item]
                    at = (q - 1) * 24 + blk * 8
                    stage[g % 4, at : at + 8, lanes] = got[g]
    tables = [split(wave_ref[pc]) for pc in range(4)]
    forced = []
    for n, g in enumerate(spread(tables, stage, 48)):
        speed = flow_ref[n, 48:72, :]
        heat = flow_ref[n, 0:24, :] + speed * g[0:24]
        field = flow_ref[n, 24:48, :] + speed * g[24:48]
        forced.append(jnp.concatenate([heat, field], axis=0))
    a, b = forced[0] + forced[1], forced[2] + forced[3]
    d, e = forced[0] - forced[1], forced[3] - forced[2]
    sides = [a + b, d + e, a - b, d - e]
    for par in range(2):
        parts = []
        for c in range(2):
            pc = par * 2 + c
            high, low = split(sides[pc])
            wave_high, wave_low = tables[pc]
            both = dot_nt(wave_high, jnp.concatenate([high, low], axis=0))
            parts.append(both[:, :48] + (both[:, 48:] + dot_nt(wave_low, high)))
        pair = jnp.concatenate(parts + [jnp.zeros((256, 32), f32)], axis=1)
        out_ref[:, par * 8 : par * 8 + 8, :] = pair.reshape(32, 8, 128)


def forcing_stage(shell, chip, link, wave, flow):
    return pl.pallas_call(
        forcing_kernel,
        in_specs=specs(1, 4),
        out_shape=near_out(32, 16, 128),
        scratch_shapes=[pltpu.VMEM((4, 48, 256), f32)],
        interpret=INTERPRET,
        compiler_params=pltpu.CompilerParams(vmem_limit_bytes=24 * 2**20),
        name="forcing",
    )(shell, near(chip), near(link), near(wave), near(flow))


def table_kernel(place_ref, map_ref, lat_ref, norm_ref, after_ref, tab_ref, last, table, ready, sems):
    legendre_table(map_ref, place_ref[0] * GROUP, lat_ref, norm_ref, table, last)
    copies = []
    for pair in range(PAIRS):
        for half in range(2):
            rows = slice(half * (DEG // 2), (half + 1) * (DEG // 2))
            for t in range(3):
                start = half * (DEG // 2) * PAIRS + pair
                turned = jnp.transpose(table[t, pl.ds(start, DEG // 2, stride=PAIRS), :])
                high, low = split(turned)
                ready[pair, t * 256 : t * 256 + 128, rows] = high
                ready[pair, t * 256 + 128 : (t + 1) * 256, rows] = low
        copy = pltpu.make_async_copy(ready.at[pair], tab_ref.at[pair], sems.at[pair])
        copy.start()
        copies.append(copy)
    for copy in copies:
        copy.wait()


def tables(place, orders, lat, norm, after):
    return pl.pallas_call(
        table_kernel,
        in_specs=specs(2, 2) + [pl.BlockSpec(memory_space=pl.ANY)],
        out_specs=[pl.BlockSpec(memory_space=pl.ANY), pl.BlockSpec(memory_space=pltpu.VMEM)],
        out_shape=[
            jax.ShapeDtypeStruct((PAIRS, 2 * NORTH, DEG), bf16),
            jax.ShapeDtypeStruct((PAIRS, NORTH), f32),
        ],
        scratch_shapes=[
            pltpu.VMEM((3, DEG * PAIRS, 128), f32),
            pltpu.VMEM((PAIRS, 2 * NORTH, DEG), bf16),
            pltpu.SemaphoreType.DMA((PAIRS,)),
        ],
        interpret=INTERPRET,
        name="legendre",
    )(place, orders, lat, norm, after)


def analysis_kernel(
    place_ref, map_ref, v_ref, temp_ref, mag_ref, sub_ref, diag_ref, sup_ref, last, tab_ref,
    out_ref, ready, sums, right, sems,
):
    first = place_ref[0] * GROUP
    copies = [
        pltpu.make_async_copy(tab_ref.at[pair], ready.at[pair], sems.at[pair]) for pair in range(PAIRS)
    ]
    for copy in copies:
        copy.start()

    def prepare():
        for par in range(2):
            halves = [
                block_swap(
                    [v_ref[half * 16 + s, par * 8 : par * 8 + 8, :] for s in range(16)], 8
                )
                for half in range(2)
            ]
            for c in range(2):
                for f in range(2):
                    tiles = []
                    for blk in range(3):
                        g = c * 6 + f * 3 + blk
                        tiles += [halves[0][g], halves[1][g]]
                    for eo in range(2):
                        at = par * 64 + (eo * 4 + f * 2 + c) * 8
                        for t in range(3):
                            mixed = tiles[t] + tiles[t + 3] if eo == 0 else tiles[t] - tiles[t + 3]
                            sums[t, at : at + 8, :] = mixed

    prepare()

    def one(step):
        slot_small, slot_large, small = pair_orders(map_ref, first, step)
        par = lax.rem(small, 2)

        def load(parity):
            start = parity * 64 + step
            return jnp.concatenate([sums[t, pl.ds(start, 8, stride=8), :] for t in range(3)], axis=1)

        value_small = load(par)
        high, low = split(jnp.concatenate([value_small, load(1 - par)], axis=0))
        zero = jnp.zeros((16, 128), bf16)
        halves = []
        for half in range(2):
            product = 0.0
            for t in range(3):
                cut = slice(t * 128, (t + 1) * 128)
                left = jnp.concatenate(
                    [
                        jnp.concatenate([high[:, cut], high[:, cut]], axis=1),
                        jnp.concatenate([low[:, cut], zero], axis=1),
                    ],
                    axis=0,
                )
                rows = slice(half * (DEG // 2), (half + 1) * (DEG // 2))
                product = product + dot_nn(left, ready[step, t * 256 : (t + 1) * 256, rows])
            halves.append(product[:16] + product[16:])
        result = jnp.concatenate(halves, axis=1)
        wide = lax.broadcasted_iota(i32, (4, DEG), 1)
        picked = jnp.where(lax.rem(wide + 1 + par, 2) == 0, result[0:4], result[4:8])
        edge_value = jnp.where(par == 1, value_small[0:4], value_small[4:8])
        edge = jnp.sum(edge_value * last[pl.ds(step, 1), :], axis=1, keepdims=True)
        tendency_small = jnp.where(wide == DEG - 1, edge, roll_lanes(picked, -1))
        tendency_small = jnp.where(wide >= small, tendency_small, 0.0)
        picked = jnp.where(lax.rem(wide, 2) == 0, result[8:12], result[12:16])
        large = DEG - 1 - small
        wide8 = jnp.concatenate([picked, picked], axis=0)
        tendency_large = jnp.where(wide >= large, pltpu.roll(wide8, large, 1)[0:4], 0.0)
        for fc in range(4):
            right[fc, pl.ds(slot_small, 1), :] = tendency_small[fc : fc + 1]
            right[fc, pl.ds(slot_large, 1), :] = tendency_large[fc : fc + 1]

    for pair in range(PAIRS):
        copies[pair].wait()
        one(pair)
    for fc in range(4):
        f, c = fc // 2, fc % 2
        base = temp_ref if f == 0 else mag_ref
        right[fc, 0:GROUP, :] = base[c * GROUP : (c + 1) * GROUP, :] + STEP * right[fc, 0:GROUP, :]
        right[fc, GROUP : GROUP + 8, :] = jnp.concatenate(
            [ref[f : f + 1, :] for ref in (sub_ref, diag_ref, sup_ref)]
            + [jnp.zeros((5, DEG), f32)],
            axis=0,
        )
    for tile in range(4):
        got = block_swap([right[fc, :, tile * 128 : (tile + 1) * 128] for fc in range(4)], 32)
        for r in range(4):
            out_ref[tile * 4 + r] = got[r]


def analysis(place, orders, v, temp, mag, sub, diag, sup, last, tab):
    return pl.pallas_call(
        analysis_kernel,
        in_specs=specs(2, 7) + [pl.BlockSpec(memory_space=pl.ANY)],
        out_shape=near_out(16, 24, 128),
        scratch_shapes=[
            pltpu.VMEM((PAIRS, 2 * NORTH, DEG), bf16),
            pltpu.VMEM((3, 128, 128), f32),
            pltpu.VMEM((4, GROUP + 8, DEG), f32),
            pltpu.SemaphoreType.DMA((PAIRS,)),
        ],
        interpret=INTERPRET,
        name="analysis",
    )(place, orders, near(v), temp, mag, sub, diag, sup, last, tab)


def solve_kernel(x_ref, out_ref):
    running = jnp.zeros((GROUP, 128), f32)
    scaled = []
    for k in range(SHELLS):
        running = x_ref[k, 0:GROUP, :] + (1.0 - x_ref[k, GROUP : GROUP + 1, :]) * running
        scaled.append(running / x_ref[k, GROUP + 1 : GROUP + 2, :])
    running = jnp.zeros((GROUP, 128), f32)
    for k in reversed(range(SHELLS)):
        running = scaled[k] + (1.0 - x_ref[k, GROUP + 2 : GROUP + 3, :]) * running
        out_ref[k] = running


def solve(x):
    return pl.pallas_call(
        solve_kernel,
        out_shape=near_out(SHELLS, GROUP, 128),
        interpret=INTERPRET,
        compiler_params=pltpu.CompilerParams(vmem_limit_bytes=8 * 2**20),
        name="radial",
    )(near(x))


def gather_kernel(x_ref, temp_ref, mag_ref):
    for tile in range(4):
        got = block_swap([x_ref[tile * 4 + r] for r in range(4)], 32)
        lanes = slice(tile * 128, (tile + 1) * 128)
        for fc in range(4):
            ref = temp_ref if fc < 2 else mag_ref
            c = fc % 2
            ref[c * GROUP : (c + 1) * GROUP, lanes] = got[fc]


def gather_stage(x):
    return pl.pallas_call(
        gather_kernel,
        out_shape=[jax.ShapeDtypeStruct((32, DEG), f32)] * 2,
        interpret=INTERPRET,
        compiler_params=pltpu.CompilerParams(vmem_limit_bytes=8 * 2**20),
        name="assemble",
    )(near(x))


def sorted_orders(orders):
    pair = orders.reshape(DEG // 2, 2)
    even = jnp.where(pair[:, 0] % 2 == 0, pair[:, 0], pair[:, 1])
    return jnp.stack([even, DEG - 1 - even])


def wave_tables(ordered):
    node = 2 * jnp.arange(QUARTER, dtype=i32) + 1
    phase = ordered[:, :, None] * node % (2 * NLON)
    angle = math.pi / NLON * phase.astype(f32)
    return jnp.stack([jnp.cos(angle), -jnp.sin(angle)], axis=1).reshape(4, DEG // 2, QUARTER)


def body(
    toroidal_stream_spectra,
    thermal_spectra,
    induction_potential,
    outward_speed_spectra,
    position_azimuth_map,
    subdiagonal_complement,
    superdiagonal_complement,
    diagonal_entries,
):
    lat, norm, per = map(jnp.asarray, host_tables())
    place = lax.axis_index("ma").reshape(1).astype(i32)
    shell = lax.axis_index("row").reshape(1).astype(i32)
    psi, temp, mag, speed = (
        a.reshape(32, DEG)
        for a in (
            toroidal_stream_spectra, thermal_spectra, induction_potential, outward_speed_spectra
        )
    )
    chunk = synthesis(place, position_azimuth_map, psi, temp, mag, speed, lat, norm)
    tab, last = tables(place, position_azimuth_map, lat, norm, chunk)
    chunk = lax.all_to_all(chunk, "ma", 0, 0, tiled=True)
    ordered = sorted_orders(position_azimuth_map)
    wave = wave_tables(ordered)
    chunk, wave, tab, last = lax.optimization_barrier((chunk, wave, tab, last))
    profiles = chunk[:, 0:16, :]
    near_pairs = [(i, i ^ 1) for i in range(SHELLS)]
    far_pairs = [(i, i + 1) for i in range(1, SHELLS - 1, 2)]
    far_pairs += [(b, a) for a, b in far_pairs]
    link = lax.ppermute(profiles, "row", far_pairs)
    chip = lax.ppermute(profiles, "row", near_pairs)
    flow = flow_stage(place, shell, chunk, wave, ordered.astype(f32), per)
    spectra = forcing_stage(shell, chip, link, wave, flow)
    spectra = lax.all_to_all(spectra, "ma", 0, 0, tiled=True)
    sub, diag, sup = (
        a.reshape(2, DEG) for a in (subdiagonal_complement, diagonal_entries, superdiagonal_complement)
    )
    right = analysis(
        place, position_azimuth_map, spectra, temp, mag, sub, diag, sup, last, tab
    )
    right = lax.all_to_all(right, "row", 0, 0, tiled=True)
    solved = lax.all_to_all(solve(right), "row", 0, 0, tiled=True)
    new_temp, new_mag = gather_stage(solved)
    shape = thermal_spectra.shape
    return new_temp.reshape(shape), new_mag.reshape(shape)


def solution(mesh):
    spectra = P(None, "row", "ma", None)
    radial = P(None, "row", None)
    in_specs = (spectra,) * 4 + (P(),) + (radial,) * 3
    return jax.shard_map(
        body, mesh=mesh, in_specs=in_specs, out_specs=(spectra, spectra), check_vma=False
    )
```
